32 devices in a mesh: rep: 16 (over z, y, core), shard: 2 (over x).
Axes of the slice: x: 2, y: 2, z: 4, core: 2. Of those that a mesh axis runs over, the one named last changes fastest.
Arguments:
- grads_query: bfloat16 [64, 960, 960], P(('rep', 'shard')), may hold values from -3000 to 3000
- master_query: float32 [960, 960], P('shard'), may hold values from -0.1875 to 0.1875
- moment_query: float32 [960, 960], P('shard'), may hold values from -6 to 6
- second_query: float32 [960, 960], P('shard'), may hold values from 0.25 to 4
- grads_keys: bfloat16 [64, 960, 320], P(('rep', 'shard')), may hold values from -3000 to 3000
- master_keys: float32 [960, 320], P('shard'), may hold values from -0.1875 to 0.1875
- moment_keys: float32 [960, 320], P('shard'), may hold values from -6 to 6
- second_keys: float32 [960, 320], P('shard'), may hold values from 0.25 to 4
Outputs:
- new_master_query: float32 [960, 960], P('shard')
- new_moment_query: float32 [960, 960], P('shard')
- new_second_query: float32 [960, 960], P('shard')
- weight_query: bfloat16 [960, 960], replicated
- new_master_keys: float32 [960, 320], P('shard')
- new_moment_keys: float32 [960, 320], P('shard')
- new_second_keys: float32 [960, 320], P('shard')
- weight_keys: bfloat16 [960, 320], replicated
The draws below stay inside these ranges and needn't reach their ends.
All inputs are finite; a program needn't handle non-finite values.
Results may differ from the reference program's by a relative error of at most 0.001.
Values may be sent and summed in bfloat16 or wider, within the bound.
A program may use at most 128 MiB of HBM per device.

```python
import math
import jax
import jax.numpy as jnp
from jax import lax

D = 960
KV = 320
MB = 2
STEP = 10
GROWS = 64


def draw_rising(key, columns):
    senders = GROWS // MB
    noise_key = jax.random.fold_in(key, 11)
    rough_key = jax.random.fold_in(key, 12)
    perm_key = jax.random.fold_in(key, 13)
    values = jax.random.truncated_normal(noise_key, -6.0, 6.0, (GROWS, D, columns), jnp.float32)
    top = 10.0
    rows = jnp.arange(D, dtype=jnp.float32) / jnp.float32(max(D - 1, 1))
    rough = jax.random.uniform(rough_key, (D,), jnp.float32, 0.7, 1.3)
    scales = jnp.exp(jnp.log(jnp.float32(top)) * rows) * rough
    pairing = jax.random.permutation(perm_key, senders).astype(jnp.int32)
    sender = jnp.arange(GROWS, dtype=jnp.int32) // MB
    target = pairing[sender]
    flat = (jnp.arange(D, dtype=jnp.int32)[:, None] * columns + jnp.arange(columns, dtype=jnp.int32)[None, :]) % senders
    heavy = jnp.where(flat[None, :, :] == target[:, None, None], jnp.float32(8.0), jnp.float32(1.0))
    return (values * heavy * scales[None, :, None]).astype(jnp.bfloat16)


def draw_grads_query(key, part):
    return draw_rising(jax.random.fold_in(key, 1), D)


def draw_grads_keys(key, part):
    return draw_rising(jax.random.fold_in(key, 2), KV)


def steps_of(key, extent, pieces, low, top_value):
    factor_of = 1.0
    for axis_at, parts in pieces:
        heights = jax.random.uniform(jax.random.fold_in(jax.random.fold_in(key, 6), axis_at), (parts,), jnp.float32, low / len(pieces), top_value / len(pieces))
        factor_of = factor_of * jnp.repeat(jnp.exp(heights), extent[axis_at] // parts).reshape((-1,) + (1,) * (len(extent) - 1 - axis_at))
    return factor_of


def gaussian(key, dims, scale, bound, cuts=(), kind=jnp.bfloat16):
    values = scale * jax.random.normal(key, dims, jnp.float32)
    if cuts:
        values = values * steps_of(key, dims, cuts, -0.22, 0.18)
    return jnp.clip(values, -bound, bound).astype(kind)


def setup_inputs(seed: int = 0) -> dict:
    streams_of = jax.random.split(jax.random.key(seed), 9)
    grads_query = draw_grads_query(jax.random.fold_in(streams_of[8], 71), 0)
    master_query = gaussian(streams_of[1], (D, D), D ** -0.5, 0.1875, ((0, 2),), jnp.float32)
    moment_query = gaussian(streams_of[2], (D, D), 1.0, 6.0, ((0, 2),), jnp.float32)
    second_query = jnp.clip(jnp.exp(math.log(4.0) - 2.7725887 * jax.random.uniform(streams_of[3], (D, D), jnp.float32) ** steps_of(streams_of[3], (D, D), ((0, 2),), -0.2, 0.2)), 0.25, 4.0)
    grads_keys = draw_grads_keys(jax.random.fold_in(streams_of[8], 71), 0)
    master_keys = gaussian(streams_of[5], (D, KV), D ** -0.5, 0.1875, ((0, 2),), jnp.float32)
    moment_keys = gaussian(streams_of[6], (D, KV), 1.0, 6.0, ((0, 2),), jnp.float32)
    second_keys = jnp.clip(jnp.exp(math.log(4.0) - 2.7725887 * jax.random.uniform(streams_of[7], (D, KV), jnp.float32) ** steps_of(streams_of[7], (D, KV), ((0, 2),), -0.2, 0.2)), 0.25, 4.0)
    return dict(grads_query=grads_query, master_query=master_query, moment_query=moment_query, second_query=second_query, grads_keys=grads_keys, master_keys=master_keys, moment_keys=moment_keys, second_keys=second_keys)


def sum_grads(grads):

    def add_one(carry, piece):
        return (carry + piece.astype(jnp.float32), None)
    start = jnp.zeros(grads.shape[1:], jnp.float32)
    total, unused = lax.scan(add_one, start, grads)
    return total

def adamw(grad_sum, master, moment, second, clip):
    grad = clip * grad_sum
    new_moment = 0.9 * moment + 0.1 * grad
    new_second = 0.999 * second + 0.001 * grad * grad
    mhat = new_moment / (1.0 - 0.9 ** STEP)
    vhat = new_second / (1.0 - 0.999 ** STEP)
    new_master = master - 0.02 * (mhat / (jnp.sqrt(vhat) + 1e-08) + 0.1 * master)
    return (new_master, new_moment, new_second, new_master.astype(jnp.bfloat16))

def reference(grads_query, master_query, moment_query, second_query, grads_keys, master_keys, moment_keys, second_keys):
    sum_query = sum_grads(grads_query)
    sum_keys = sum_grads(grads_keys)
    total = jnp.sum(sum_query * sum_query) + jnp.sum(sum_keys * sum_keys)
    limit = jnp.sqrt(jnp.float32(D * D + D * KV))
    clip = jnp.minimum(jnp.float32(1.0), limit / (jnp.sqrt(total) + 1e-06))
    query_out = adamw(sum_query, master_query, moment_query, second_query, clip)
    keys_out = adamw(sum_keys, master_keys, moment_keys, second_keys, clip)
    return (query_out[0], query_out[1], query_out[2], query_out[3], keys_out[0], keys_out[1], keys_out[2], keys_out[3])
```

```python
import functools

import jax
import jax.numpy as jnp
from jax import lax
from jax.experimental import pallas as pl
from jax.experimental.pallas import tpu as pltpu
from jax.sharding import PartitionSpec as P

D = 960
KV = 320
STEP = 10
CORES = 2
RT = 16
WIDE = D + KV
MAIN = KV // 128 * 128
MESH = pl.DeviceIdType.MESH
F32 = jnp.float32
BF16 = jnp.bfloat16


def join(q, k):
    return jnp.concatenate([q, k[:, MAIN:], k[:, :MAIN]], axis=1)


def split(wide):
    rest = KV - MAIN
    return wide[:, :D], jnp.concatenate([wide[:, D + rest :], wide[:, D : D + rest]], axis=1)


def adamw(grad_sum, master, moment, second, clip):
    grad = clip * grad_sum
    new_moment = 0.9 * moment + 0.1 * grad
    new_second = 0.999 * second + 0.001 * grad * grad
    mhat = new_moment / (1.0 - 0.9**STEP)
    vhat = new_second / (1.0 - 0.999**STEP)
    new_master = master - 0.02 * (mhat / (jnp.sqrt(vhat) + 1e-08) + 0.1 * master)
    return new_master, new_moment, new_second


def kernel(
    zy_n, np_n, pr, rpc,
    gq_hbm, mq_hbm, oq_hbm, sq_hbm, gk_hbm, mk_hbm, ok_hbm, sk_hbm,
    nmq_hbm, noq_hbm, nsq_hbm, nmk_hbm, nok_hbm, nsk_hbm, w_hbm,
    gq, gk, mq, oq, sq, mk, ok, sk,
    cs, cr, xs, xr, zs, zr, own, g, w, norm, normx,
    in_sem, st_sem, out_sem, w_sem,
    cs_s, cr_s, xs_s, xr_s, zs_s, zr_s,
    ags_s, agr_s, fs_s, fr_s, ws_s, wr_s, vs_s, vr_s, ns_s, nr_s,
):
    rep = lax.axis_index("rep")
    x = lax.axis_index("shard")
    c = lax.rem(rep, CORES)
    zy = lax.div(rep, CORES)
    half = CORES * rpc
    core_dev = (zy * CORES + 1 - c, x)
    x_dev = (rep, 1 - x)
    tiles = pr // RT

    def peer(j):
        return lax.rem(zy + j, zy_n)

    def zy_dev(q):
        return (q * CORES + c, x)

    def piece(k):
        return lax.rem(zy + 1 + k, np_n)

    def rcopy(src, dst, s, r, dev):
        return pltpu.make_async_remote_copy(
            src_ref=src, dst_ref=dst, send_sem=s, recv_sem=r, device_id=dev, device_id_type=MESH
        )

    grads_in = [
        pltpu.make_async_copy(gq_hbm, gq, in_sem.at[0]),
        pltpu.make_async_copy(gk_hbm, gk, in_sem.at[1]),
    ]
    for one in grads_in:
        one.start()
    states = [(mq_hbm, mq), (oq_hbm, oq), (sq_hbm, sq), (mk_hbm, mk), (ok_hbm, ok), (sk_hbm, sk)]
    states_in = [
        pltpu.make_async_copy(src, dst, st_sem.at[i]) for i, (src, dst) in enumerate(states)
    ]
    for one in states_in:
        one.start()

    barrier = pltpu.get_barrier_semaphore()
    pl.semaphore_signal(barrier, inc=1, device_id=core_dev, device_id_type=MESH)
    pl.semaphore_signal(barrier, inc=1, device_id=x_dev, device_id_type=MESH)

    @pl.loop(1, zy_n)
    def _(j):
        pl.semaphore_signal(barrier, inc=1, device_id=zy_dev(peer(j)), device_id_type=MESH)

    for one in grads_in:
        one.wait()
    pl.semaphore_wait(barrier, zy_n + 1)

    def rows_of(p, t):
        return jnp.minimum(p * pr + t * RT, rpc - RT)

    def lsum(xh, core, p, t):
        row = pl.ds(pl.multiple_of(xh * half + core * rpc + rows_of(p, t), RT), RT)
        q = gq[0, row, :].astype(F32)
        k = gk[0, row, :].astype(F32)
        for m in range(1, gq.shape[0]):
            q = q + gq[m, row, :].astype(F32)
            k = k + gk[m, row, :].astype(F32)
        return join(q, k)

    def tile(t):
        return pl.ds(t * RT, RT)

    def core_copy(k):
        return rcopy(cs.at[k], cr.at[k], cs_s.at[k], cr_s.at[k], core_dev)

    def x_copy(k):
        return rcopy(xs.at[k], xr.at[k], xs_s.at[k], xr_s.at[k], x_dev)

    def zy_copy(k):
        return rcopy(zs.at[k], zr.at[zy], zs_s.at[k], zr_s.at[zy], zy_dev(piece(k)))

    def zy_arrival(s):
        return rcopy(zs.at[0], zr.at[s], zs_s.at[0], zr_s.at[s], zy_dev(s))

    @pl.loop(0, np_n)
    def _(k):
        p = piece(k)
        for xh in range(2):
            for t in range(tiles):
                cs[k, xh, tile(t), :] = lsum(xh, 1 - c, p, t).astype(BF16)
        core_copy(k).start()

    @pl.loop(0, np_n)
    def _(k):
        p = piece(k)
        core_copy(k).wait_recv()
        for t in range(tiles):
            part = lsum(1 - x, c, p, t) + cr[k, 1 - x, tile(t), :].astype(F32)
            xs[k, tile(t), :] = part.astype(BF16)
        x_copy(k).start()

    @pl.loop(0, np_n)
    def _(k):
        p = piece(k)
        x_copy(k).wait_recv()
        for t in range(tiles):
            part = lsum(x, c, p, t) + cr[k, x, tile(t), :].astype(F32)
            part = part + xr[k, tile(t), :].astype(F32)

            @pl.when(p == zy)
            def _():
                own[tile(t), :] = part

            @pl.when(p != zy)
            def _():
                zs[k, tile(t), :] = part.astype(BF16)

        @pl.when(p != zy)
        def _():
            zy_copy(k).start()

    def norm_copy(i, dev):
        return rcopy(norm.at[i], normx.at[i], ns_s.at[i], nr_s.at[i], dev)

    def fold(a):
        total = jnp.zeros((8, 128), F32)
        for r in range(0, a.shape[0], 8):
            for l in range(0, a.shape[1], 128):
                total = total + a[r : r + 8, l : l + 128]
        return total

    def gather_copy(j):
        return rcopy(g.at[c, zy], g.at[c, zy], ags_s.at[j], agr_s.at[zy], zy_dev(peer(j)))

    def gather_arrival(p):
        return rcopy(g.at[c, p], g.at[c, p], ags_s.at[0], agr_s.at[p], zy_dev(p))

    def forward(core, p):
        return rcopy(g.at[core, p], g.at[core, p], fs_s.at[p], fr_s.at[p], core_dev)

    norm[0] = jnp.zeros((8, 128), F32)

    @pl.when(zy < np_n)
    def _():
        @pl.loop(1, zy_n)
        def _(j):
            zy_arrival(lax.rem(zy + zy_n - j, zy_n)).wait_recv()

        total = jnp.zeros((8, 128), F32)
        for t in range(tiles):

            def add(j, acc):
                return acc + zr[peer(j), tile(t), :].astype(F32)

            acc = lax.fori_loop(1, zy_n, add, own[tile(t), :])
            g[c, zy, tile(t), :] = acc.astype(BF16)
            valid = (zy * pr + t * RT < rpc).astype(F32)
            total = total + fold(acc * acc) * valid
        norm[0] = total

    norm_copy(0, core_dev).start()

    @pl.when(zy < np_n)
    def _():
        forward(c, zy).start()

        @pl.loop(1, zy_n)
        def _(j):
            gather_copy(j).start()

    norm_copy(0, core_dev).wait_recv()
    norm[1] = norm[0] + normx[0]
    norm_copy(1, x_dev).start()
    norm_copy(1, x_dev).wait_recv()
    norm[2] = norm[1] + normx[1]

    def norm_out(j):
        return rcopy(norm.at[2], normx.at[2 + zy], ns_s.at[2 + j], nr_s.at[2 + zy], zy_dev(peer(j)))

    def norm_in(s):
        return rcopy(norm.at[2], normx.at[2 + s], ns_s.at[2], nr_s.at[2 + s], zy_dev(s))

    @pl.loop(1, zy_n)
    def _(j):
        norm_out(j).start()

    normx[2 + zy] = norm[2]

    @pl.loop(1, zy_n)
    def _(j):
        norm_in(peer(j)).wait_recv()

    total = lax.fori_loop(0, zy_n, lambda s, acc: acc + normx[2 + s], jnp.zeros((8, 128), F32))
    total = jnp.sum(jnp.sum(total, axis=1, keepdims=True), axis=0, keepdims=True)
    limit = jnp.sqrt(jnp.full((1, 1), D * D + D * KV, F32))
    clip = jnp.minimum(1.0, limit / (jnp.sqrt(total) + 1e-06))

    for one in states_in:
        one.wait()

    def weights_over(p):
        return rcopy(w.at[x, c, p], w.at[x, c, p], ws_s.at[p], wr_s.at[p], x_dev)

    def weights_in(p):
        return rcopy(w.at[1 - x, c, p], w.at[1 - x, c, p], ws_s.at[p], wr_s.at[p], x_dev)

    def weights_forward(p):
        return rcopy(w.at[1 - x, c, p], w.at[1 - x, c, p], vs_s.at[p], vr_s.at[p], core_dev)

    def weights_last(p):
        return rcopy(w.at[1 - x, 1 - c, p], w.at[1 - x, 1 - c, p], vs_s.at[p], vr_s.at[p], core_dev)

    def update(core, p):
        for t in range(tiles):
            row = pl.ds(pl.multiple_of(core * rpc + rows_of(p, t), RT), RT)

            @pl.when(p * pr + t * RT < rpc)
            def _():
                gsq, gsk = split(g[core, p, tile(t), :].astype(F32))
                m, o, s = adamw(gsq, mq[row, :], oq[row, :], sq[row, :], clip)
                mq[row, :] = m
                oq[row, :] = o
                sq[row, :] = s
                km, ko, ks = adamw(gsk, mk[row, :], ok[row, :], sk[row, :], clip)
                mk[row, :] = km
                ok[row, :] = ko
                sk[row, :] = ks
                w[x, core, p, tile(t), :] = join(m, km).astype(BF16)

    outs = [(mq, nmq_hbm), (oq, noq_hbm), (sq, nsq_hbm), (mk, nmk_hbm), (ok, nok_hbm), (sk, nsk_hbm)]

    def out_copies(core, n):
        row = pl.ds(pl.multiple_of(core * rpc, RT), rpc)
        return [
            pltpu.make_async_copy(src.at[row, :], dst.at[row, :], out_sem.at[n, i])
            for i, (src, dst) in enumerate(outs)
        ]

    @pl.loop(0, np_n)
    def _(k):
        p = lax.rem(zy + np_n - k, np_n)

        @pl.when(p != zy)
        def _():
            gather_arrival(p).wait_recv()
            forward(c, p).start()

        update(c, p)
        weights_over(p).start()

    mine_out = out_copies(c, 0)
    for one in mine_out:
        one.start()

    @pl.loop(0, np_n)
    def _(k):
        p = lax.rem(zy + np_n - k, np_n)
        forward(1 - c, p).wait_recv()
        update(1 - c, p)

    other_out = out_copies(1 - c, 1)
    for one in other_out:
        one.start()
    w_own = pltpu.make_async_copy(w.at[x], w_hbm.at[x], w_sem.at[0])
    w_own.start()

    @pl.loop(0, np_n)
    def _(k):
        p = lax.rem(zy + np_n - k, np_n)
        weights_in(p).wait_recv()
        weights_forward(p).start()

    w_c = pltpu.make_async_copy(w.at[1 - x, c], w_hbm.at[1 - x, c], w_sem.at[1])
    w_c.start()

    @pl.loop(0, np_n)
    def _(k):
        weights_last(lax.rem(zy + np_n - k, np_n)).wait_recv()

    w_o = pltpu.make_async_copy(w.at[1 - x, 1 - c], w_hbm.at[1 - x, 1 - c], w_sem.at[2])
    w_o.start()

    @pl.loop(0, np_n)
    def _(k):
        core_copy(k).wait_send()
        x_copy(k).wait_send()

        @pl.when(piece(k) != zy)
        def _():
            zy_copy(k).wait_send()

        forward(c, k).wait_send()
        weights_over(k).wait_send()
        weights_forward(k).wait_send()

    @pl.when(zy < np_n)
    def _():
        @pl.loop(1, zy_n)
        def _(j):
            gather_copy(j).wait_send()

    @pl.loop(1, zy_n)
    def _(j):
        norm_out(j).wait_send()

    norm_copy(0, core_dev).wait_send()
    norm_copy(1, x_dev).wait_send()
    for one in mine_out + other_out + [w_own, w_c, w_o]:
        one.wait()


def local(zy_n, grads_query, master_query, moment_query, second_query, grads_keys, master_keys, moment_keys, second_keys):
    half = master_query.shape[0]
    rpc = half // CORES
    tiles_all = rpc // RT
    per = -(-tiles_all // zy_n)
    np_n = -(-tiles_all // per)
    pr = per * RT
    states = [master_query, moment_query, second_query, master_keys, moment_keys, second_keys]
    sem = lambda n: pltpu.SemaphoreType.DMA((n,))
    any_spec = pl.BlockSpec(memory_space=pl.ANY)
    outs = pl.pallas_call(
        functools.partial(kernel, zy_n, np_n, pr, rpc),
        out_shape=[jax.ShapeDtypeStruct(a.shape, F32) for a in states]
        + [jax.ShapeDtypeStruct((2, CORES, np_n, pr, WIDE), BF16)],
        in_specs=[any_spec] * 8,
        out_specs=[any_spec] * 7,
        scratch_shapes=[
            pltpu.VMEM(grads_query.shape, BF16),
            pltpu.VMEM(grads_keys.shape, BF16),
        ]
        + [pltpu.VMEM(a.shape, F32) for a in states]
        + [
            pltpu.VMEM((np_n, 2, pr, WIDE), BF16),
            pltpu.VMEM((np_n, 2, pr, WIDE), BF16),
            pltpu.VMEM((np_n, pr, WIDE), BF16),
            pltpu.VMEM((np_n, pr, WIDE), BF16),
            pltpu.VMEM((np_n, pr, WIDE), BF16),
            pltpu.VMEM((zy_n, pr, WIDE), BF16),
            pltpu.VMEM((pr, WIDE), F32),
            pltpu.VMEM((CORES, np_n, pr, WIDE), BF16),
            pltpu.VMEM((2, CORES, np_n, pr, WIDE), BF16),
            pltpu.VMEM((3, 8, 128), F32),
            pltpu.VMEM((2 + zy_n, 8, 128), F32),
            sem(2), sem(6), pltpu.SemaphoreType.DMA((2, 6)), sem(3),
            sem(np_n), sem(np_n), sem(np_n), sem(np_n), sem(np_n), sem(zy_n),
            sem(zy_n), sem(np_n), sem(np_n), sem(np_n),
            sem(np_n), sem(np_n), sem(np_n), sem(np_n), sem(2 + zy_n), sem(2 + zy_n),
        ],
        compiler_params=pltpu.CompilerParams(
            collective_id=0, has_side_effects=True, vmem_limit_bytes=56 << 20
        ),
    )(grads_query, master_query, moment_query, second_query, grads_keys, master_keys, moment_keys, second_keys)
    weights = outs[6].reshape(2, CORES, np_n * pr, WIDE)[:, :, :rpc, :].reshape(2 * half, WIDE)
    weight_query, weight_keys = split(weights)
    return (*outs[0:3], weight_query, *outs[3:6], weight_keys)


def solution(mesh):
    zy_n = mesh.shape["rep"] // CORES
    rows = P("shard", None)
    grads = P(("rep", "shard"), None, None)
    in_specs = (grads, rows, rows, rows, grads, rows, rows, rows)
    out_specs = (rows, rows, rows, P(), rows, rows, rows, P())
    return jax.shard_map(
        functools.partial(local, zy_n), mesh=mesh, in_specs=in_specs, out_specs=out_specs, check_vma=False
    )
```

```python
import functools

import jax
import jax.numpy as jnp
from jax import lax
from jax.experimental import pallas as pl
from jax.experimental.pallas import tpu as pltpu
from jax.sharding import PartitionSpec as P

D = 960
KV = 320
STEP = 10
CORES = 2
RT = 16
WIDE = D + KV
MAIN = KV // 128 * 128
MESH = pl.DeviceIdType.MESH
F32 = jnp.float32
BF16 = jnp.bfloat16


def join(q, k):
    return jnp.concatenate([q, k[:, MAIN:], k[:, :MAIN]], axis=1)


def split(wide):
    rest = KV - MAIN
    return wide[:, :D], jnp.concatenate([wide[:, D + rest :], wide[:, D : D + rest]], axis=1)


def adamw(grad_sum, master, moment, second, clip):
    grad = clip * grad_sum
    new_moment = 0.9 * moment + 0.1 * grad
    new_second = 0.999 * second + 0.001 * grad * grad
    mhat = new_moment / (1.0 - 0.9**STEP)
    vhat = new_second / (1.0 - 0.999**STEP)
    new_master = master - 0.02 * (mhat / (jnp.sqrt(vhat) + 1e-08) + 0.1 * master)
    return new_master, new_moment, new_second


def kernel(
    zy_n, np_n, pr, rpc,
    gq_hbm, mq_hbm, oq_hbm, sq_hbm, gk_hbm, mk_hbm, ok_hbm, sk_hbm,
    nmq_hbm, noq_hbm, nsq_hbm, nmk_hbm, nok_hbm, nsk_hbm, w_hbm,
    gq, gk, mq, oq, sq, mkt, okt, skt, mk, ok, sk, lk,
    cs, cr, xs, xr, zs, zr, own, g, w, norm, normx,
    in_sem, st_sem, out_sem, w_sem,
    cs_s, cr_s, xs_s, xr_s, zs_s, zr_s,
    ags_s, agr_s, is_s, fs_s, fr_s, ws_s, wr_s, vs_s, vr_s, ns_s, nr_s,
):
    rep = lax.axis_index("rep")
    x = lax.axis_index("shard")
    c = lax.rem(rep, CORES)
    zy = lax.div(rep, CORES)
    half = CORES * rpc
    core_dev = (zy * CORES + 1 - c, x)
    x_dev = (rep, 1 - x)
    tiles = pr // RT

    def peer(j):
        return lax.rem(zy + j, zy_n)

    def zy_dev(q):
        return (q * CORES + c, x)

    def piece(k):
        return lax.rem(zy + 1 + k, np_n)

    def rcopy(src, dst, s, r, dev):
        return pltpu.make_async_remote_copy(
            src_ref=src, dst_ref=dst, send_sem=s, recv_sem=r, device_id=dev, device_id_type=MESH
        )

    inner = lax.rem(zy, 2)
    outer = lax.div(zy, 2)
    outer_n = zy_n // 2

    def grads_copy(i, xh, core):
        row = pl.ds(pl.multiple_of(xh * half + core * rpc, RT), rpc)
        return pltpu.make_async_copy(gq_hbm.at[:, row, :], gq.at[:, row, :], in_sem.at[i])

    keys_in = pltpu.make_async_copy(gk_hbm, gk, in_sem.at[4])
    grads_in = [
        grads_copy(0, 0, 1 - c),
        grads_copy(1, 1, 1 - c),
        grads_copy(2, 1 - x, c),
        grads_copy(3, x, c),
    ]
    keys_in.start()
    for one in grads_in:
        one.start()
    states = [(mq_hbm, mq), (oq_hbm, oq), (sq_hbm, sq), (mk_hbm, mkt), (ok_hbm, okt), (sk_hbm, skt)]
    states_in = [
        pltpu.make_async_copy(src, dst, st_sem.at[i]) for i, (src, dst) in enumerate(states)
    ]

    barrier = pltpu.get_barrier_semaphore()
    pl.semaphore_signal(barrier, inc=1, device_id=core_dev, device_id_type=MESH)
    pl.semaphore_signal(barrier, inc=1, device_id=x_dev, device_id_type=MESH)

    @pl.loop(1, zy_n)
    def _(j):
        pl.semaphore_signal(barrier, inc=1, device_id=zy_dev(peer(j)), device_id_type=MESH)

    keys_in.wait()
    for lane in range(0, gk.shape[2], 128):
        lanes = slice(lane, min(lane + 128, gk.shape[2]))
        k = gk[0, :, lanes].astype(F32)
        for m in range(1, gk.shape[0]):
            k = k + gk[m, :, lanes].astype(F32)
        lk[lanes, :] = k.T
    grads_in[0].wait()
    grads_in[1].wait()
    pl.semaphore_wait(barrier, zy_n + 1)

    def rows_of(p, t):
        return jnp.minimum(p * pr + t * RT, rpc - RT)

    def lsum(xh, core, p, t):
        row = pl.ds(pl.multiple_of(xh * half + core * rpc + rows_of(p, t), RT), RT)
        q = gq[0, row, :].astype(F32)
        for m in range(1, gq.shape[0]):
            q = q + gq[m, row, :].astype(F32)
        return join(q, lk[row, :])

    def tile(t):
        return pl.ds(t * RT, RT)

    def core_copy(k):
        return rcopy(cs.at[k], cr.at[k], cs_s.at[k], cr_s.at[k], core_dev)

    def x_copy(k):
        return rcopy(xs.at[k], xr.at[k], xs_s.at[k], xr_s.at[k], x_dev)

    def zy_copy(k):
        return rcopy(zs.at[k], zr.at[zy], zs_s.at[k], zr_s.at[zy], zy_dev(piece(k)))

    def zy_arrival(s):
        return rcopy(zs.at[0], zr.at[s], zs_s.at[0], zr_s.at[s], zy_dev(s))

    @pl.loop(0, np_n)
    def _(k):
        p = piece(k)
        for xh in range(2):
            for t in range(tiles):
                cs[k, xh, tile(t), :] = lsum(xh, 1 - c, p, t).astype(BF16)
        core_copy(k).start()

    for one in states_in:
        one.start()
    grads_in[2].wait()
    grads_in[3].wait()

    @pl.loop(0, np_n)
    def _(k):
        p = piece(k)
        core_copy(k).wait_recv()
        for t in range(tiles):
            part = lsum(1 - x, c, p, t) + cr[k, 1 - x, tile(t), :].astype(F32)
            xs[k, tile(t), :] = part.astype(BF16)
        x_copy(k).start()

    for i, (src, dst) in enumerate([(mkt, mk), (okt, ok), (skt, sk)]):
        states_in[3 + i].wait()
        dst[...] = src[...].T

    @pl.loop(0, np_n)
    def _(k):
        p = piece(k)
        x_copy(k).wait_recv()
        for t in range(tiles):
            part = lsum(x, c, p, t) + cr[k, x, tile(t), :].astype(F32)
            part = part + xr[k, tile(t), :].astype(F32)

            @pl.when(p == zy)
            def _():
                own[tile(t), :] = part

            @pl.when(p != zy)
            def _():
                zs[k, tile(t), :] = part.astype(BF16)

        @pl.when(p != zy)
        def _():
            zy_copy(k).start()

    def fold(a):
        total = jnp.zeros((8, 128), F32)
        for r in range(0, a.shape[0], 8):
            for l in range(0, a.shape[1], 128):
                total = total + a[r : r + 8, l : l + 128]
        return total

    def gather_copy(j):
        to = lax.rem(outer + j, outer_n) * 2 + inner
        return rcopy(g.at[c, zy], g.at[c, zy], ags_s.at[j], agr_s.at[zy], zy_dev(to))

    def inner_copy(p):
        return rcopy(g.at[c, p], g.at[c, p], is_s.at[p], agr_s.at[p], zy_dev(zy + 1 - 2 * inner))

    def gather_arrival(p):
        return rcopy(g.at[c, p], g.at[c, p], ags_s.at[0], agr_s.at[p], zy_dev(p))

    def forward(core, p):
        return rcopy(g.at[core, p], g.at[core, p], fs_s.at[p], fr_s.at[p], core_dev)

    norm[0] = jnp.zeros((8, 128), F32)

    @pl.when(zy < np_n)
    def _():
        @pl.loop(1, zy_n)
        def _(j):
            zy_arrival(lax.rem(zy + zy_n - j, zy_n)).wait_recv()

        total = jnp.zeros((8, 128), F32)
        for t in range(tiles):

            def add(j, acc):
                return acc + zr[peer(j), tile(t), :].astype(F32)

            acc = lax.fori_loop(1, zy_n, add, own[tile(t), :])
            g[c, zy, tile(t), :] = acc.astype(BF16)
            valid = (zy * pr + t * RT < rpc).astype(F32)
            total = total + fold(acc * acc) * valid
        norm[0] = total

    def norm_out(j):
        return rcopy(norm.at[0], normx.at[2 + zy], ns_s.at[2 + j], nr_s.at[2 + zy], zy_dev(peer(j)))

    def norm_in(q):
        return rcopy(norm.at[0], normx.at[2 + q], ns_s.at[2], nr_s.at[2 + q], zy_dev(q))

    @pl.loop(1, zy_n)
    def _(j):
        norm_out(j).start()

    @pl.when(zy < np_n)
    def _():
        @pl.loop(1, outer_n)
        def _(j):
            gather_copy(j).start()

        inner_copy(zy).start()

    normx[2 + zy] = norm[0]

    @pl.loop(1, zy_n)
    def _(j):
        norm_in(peer(j)).wait_recv()

    norm[1] = lax.fori_loop(0, zy_n, lambda q, acc: acc + normx[2 + q], jnp.zeros((8, 128), F32))
    norm_first = rcopy(norm.at[1], normx.at[0], ns_s.at[0], nr_s.at[0], core_dev)
    norm_first.start()

    @pl.when(zy < np_n)
    def _():
        forward(c, zy).start()

    norm_first.wait_recv()
    norm[2] = norm[1] + normx[0]
    norm_last = rcopy(norm.at[2], normx.at[1], ns_s.at[1], nr_s.at[1], x_dev)
    norm_last.start()
    norm_last.wait_recv()
    total = norm[2] + normx[1]
    total = jnp.sum(jnp.sum(total, axis=1, keepdims=True), axis=0, keepdims=True)
    limit = jnp.sqrt(jnp.full((1, 1), D * D + D * KV, F32))
    clip = jnp.minimum(1.0, limit / (jnp.sqrt(total) + 1e-06))

    for one in states_in[:3]:
        one.wait()

    def weights_over(p):
        return rcopy(w.at[x, c, p], w.at[x, c, p], ws_s.at[p], wr_s.at[p], x_dev)

    def weights_in(p):
        return rcopy(w.at[1 - x, c, p], w.at[1 - x, c, p], ws_s.at[p], wr_s.at[p], x_dev)

    def weights_forward(p):
        return rcopy(w.at[1 - x, c, p], w.at[1 - x, c, p], vs_s.at[p], vr_s.at[p], core_dev)

    def weights_last(p):
        return rcopy(w.at[1 - x, 1 - c, p], w.at[1 - x, 1 - c, p], vs_s.at[p], vr_s.at[p], core_dev)

    def update(core, p):
        for t in range(tiles):
            row = pl.ds(pl.multiple_of(core * rpc + rows_of(p, t), RT), RT)

            @pl.when(p * pr + t * RT < rpc)
            def _():
                gsq, gsk = split(g[core, p, tile(t), :].astype(F32))
                m, o, s = adamw(gsq, mq[row, :], oq[row, :], sq[row, :], clip)
                mq[row, :] = m
                oq[row, :] = o
                sq[row, :] = s
                km, ko, ks = adamw(gsk, mk[row, :], ok[row, :], sk[row, :], clip)
                mk[row, :] = km
                ok[row, :] = ko
                sk[row, :] = ks
                w[x, core, p, tile(t), :] = join(m, km).astype(BF16)

    def out_copies(core, n):
        row = pl.ds(pl.multiple_of(core * rpc, RT), rpc)
        return [
            pltpu.make_async_copy(src.at[row, :], dst.at[row, :], out_sem.at[n, i])
            for i, (src, dst) in enumerate([(mq, nmq_hbm), (oq, noq_hbm), (sq, nsq_hbm)])
        ]

    def use(p):
        update(c, p)
        weights_over(p).start()

    @pl.when(zy < np_n)
    def _():
        use(zy)

    @pl.loop(1, outer_n)
    def _(j):
        p = lax.rem(outer + outer_n - j, outer_n) * 2 + inner

        @pl.when(p < np_n)
        def _():
            gather_arrival(p).wait_recv()
            inner_copy(p).start()
            forward(c, p).start()
            use(p)

    @pl.loop(0, outer_n)
    def _(j):
        p = lax.rem(outer + outer_n - j, outer_n) * 2 + 1 - inner

        @pl.when(p < np_n)
        def _():
            gather_arrival(p).wait_recv()
            forward(c, p).start()
            use(p)

    mine_out = out_copies(c, 0)
    for one in mine_out:
        one.start()

    @pl.loop(0, np_n)
    def _(k):
        p = lax.rem(zy + np_n - k, np_n)
        forward(1 - c, p).wait_recv()
        update(1 - c, p)

    other_out = out_copies(1 - c, 1)
    for one in other_out:
        one.start()
    keys_out = []
    for i, (src, mid, dst) in enumerate([(mk, mkt, nmk_hbm), (ok, okt, nok_hbm), (sk, skt, nsk_hbm)]):
        mid[...] = src[...].T
        one = pltpu.make_async_copy(mid, dst, out_sem.at[0, 3 + i])
        one.start()
        keys_out.append(one)
    w_own = pltpu.make_async_copy(w.at[x], w_hbm.at[x], w_sem.at[0])
    w_own.start()

    @pl.loop(0, np_n)
    def _(k):
        p = lax.rem(zy + np_n - k, np_n)
        weights_in(p).wait_recv()
        weights_forward(p).start()

    w_c = pltpu.make_async_copy(w.at[1 - x, c], w_hbm.at[1 - x, c], w_sem.at[1])
    w_c.start()

    @pl.loop(0, np_n)
    def _(k):
        weights_last(lax.rem(zy + np_n - k, np_n)).wait_recv()

    w_o = pltpu.make_async_copy(w.at[1 - x, 1 - c], w_hbm.at[1 - x, 1 - c], w_sem.at[2])
    w_o.start()

    @pl.loop(0, np_n)
    def _(k):
        core_copy(k).wait_send()
        x_copy(k).wait_send()

        @pl.when(piece(k) != zy)
        def _():
            zy_copy(k).wait_send()

        forward(c, k).wait_send()
        weights_over(k).wait_send()
        weights_forward(k).wait_send()

        @pl.when(lax.rem(k, 2) == inner)
        def _():
            inner_copy(k).wait_send()

    @pl.when(zy < np_n)
    def _():
        @pl.loop(1, outer_n)
        def _(j):
            gather_copy(j).wait_send()

    @pl.loop(1, zy_n)
    def _(j):
        norm_out(j).wait_send()

    norm_first.wait_send()
    norm_last.wait_send()
    for one in mine_out + other_out + keys_out + [w_own, w_c, w_o]:
        one.wait()


def local(zy_n, grads_query, master_query, moment_query, second_query, grads_keys, master_keys, moment_keys, second_keys):
    half = master_query.shape[0]
    rpc = half // CORES
    tiles_all = rpc // RT
    per = -(-tiles_all // zy_n)
    np_n = -(-tiles_all // per)
    pr = per * RT
    keys = [master_keys, moment_keys, second_keys]
    states = [master_query, moment_query, second_query] + [a.T for a in keys]
    grads_keys = grads_keys.transpose(0, 2, 1)
    sem = lambda n: pltpu.SemaphoreType.DMA((n,))
    any_spec = pl.BlockSpec(memory_space=pl.ANY)
    outs = pl.pallas_call(
        functools.partial(kernel, zy_n, np_n, pr, rpc),
        out_shape=[jax.ShapeDtypeStruct(a.shape, F32) for a in states]
        + [jax.ShapeDtypeStruct((2, CORES, np_n, pr, WIDE), BF16)],
        in_specs=[any_spec] * 8,
        out_specs=[any_spec] * 7,
        scratch_shapes=[
            pltpu.VMEM(grads_query.shape, BF16),
            pltpu.VMEM(grads_keys.shape, BF16),
        ]
        + [pltpu.VMEM(a.shape, F32) for a in states + keys]
        + [pltpu.VMEM((grads_keys.shape[2], grads_keys.shape[1]), F32)]
        + [
            pltpu.VMEM((np_n, 2, pr, WIDE), BF16),
            pltpu.VMEM((np_n, 2, pr, WIDE), BF16),
            pltpu.VMEM((np_n, pr, WIDE), BF16),
            pltpu.VMEM((np_n, pr, WIDE), BF16),
            pltpu.VMEM((np_n, pr, WIDE), BF16),
            pltpu.VMEM((zy_n, pr, WIDE), BF16),
            pltpu.VMEM((pr, WIDE), F32),
            pltpu.VMEM((CORES, np_n, pr, WIDE), BF16),
            pltpu.VMEM((2, CORES, np_n, pr, WIDE), BF16),
            pltpu.VMEM((3, 8, 128), F32),
            pltpu.VMEM((2 + zy_n, 8, 128), F32),
            sem(5), sem(6), pltpu.SemaphoreType.DMA((2, 6)), sem(3),
            sem(np_n), sem(np_n), sem(np_n), sem(np_n), sem(np_n), sem(zy_n),
            sem(zy_n), sem(np_n), sem(np_n), sem(np_n), sem(np_n),
            sem(np_n), sem(np_n), sem(np_n), sem(np_n), sem(2 + zy_n), sem(2 + zy_n),
        ],
        compiler_params=pltpu.CompilerParams(
            collective_id=0, has_side_effects=True, vmem_limit_bytes=56 << 20
        ),
    )(grads_query, *states[:3], grads_keys, *states[3:])
    weights = outs[6].reshape(2, CORES, np_n * pr, WIDE)[:, :, :rpc, :].reshape(2 * half, WIDE)
    weight_query, weight_keys = split(weights)
    return (*outs[0:3], weight_query, *[a.T for a in outs[3:6]], weight_keys)


def solution(mesh):
    zy_n = mesh.shape["rep"] // CORES
    rows = P("shard", None)
    grads = P(("rep", "shard"), None, None)
    in_specs = (grads, rows, rows, rows, grads, rows, rows, rows)
    out_specs = (rows, rows, rows, P(), rows, rows, rows, P())
    return jax.shard_map(
        functools.partial(local, zy_n), mesh=mesh, in_specs=in_specs, out_specs=out_specs, check_vma=False
    )
```

```python
import functools

import jax
import jax.numpy as jnp
from jax import lax
from jax.experimental import pallas as pl
from jax.experimental.pallas import tpu as pltpu
from jax.sharding import PartitionSpec as P

D = 960
KV = 320
STEP = 10
CORES = 2
RT = 16
WIDE = D + KV
MAIN = KV // 128 * 128
MESH = pl.DeviceIdType.MESH
F32 = jnp.float32
BF16 = jnp.bfloat16


def join(q, k):
    return jnp.concatenate([q, k[:, MAIN:], k[:, :MAIN]], axis=1)


def split(wide):
    rest = KV - MAIN
    return wide[:, :D], jnp.concatenate([wide[:, D + rest :], wide[:, D : D + rest]], axis=1)


def adamw(grad_sum, master, moment, second, clip):
    grad = clip * grad_sum
    new_moment = 0.9 * moment + 0.1 * grad
    new_second = 0.999 * second + 0.001 * grad * grad
    mhat = new_moment * (1.0 / (1.0 - 0.9**STEP))
    vhat = new_second * (1.0 / (1.0 - 0.999**STEP))
    new_master = master - 0.02 * (mhat / (jnp.sqrt(vhat) + 1e-08) + 0.1 * master)
    return new_master, new_moment, new_second


def kernel(
    zy_n, np_n, pr, rpc,
    gq_hbm, mq_hbm, oq_hbm, sq_hbm, gk_hbm, mk_hbm, ok_hbm, sk_hbm,
    g_hbm, w_hbm, clip_ref,
    gq, gk, mq, oq, sq, mkt, okt, skt, mk, ok, sk, lk,
    cs, cr, xs, xr, zs, zr, own, g, w, norm, normx,
    in_sem, st_sem, w_sem,
    cs_s, cr_s, xs_s, xr_s, zs_s, zr_s,
    ags_s, agr_s, is_s, fs_s, fr_s, ws_s, wr_s, vs_s, vr_s, us_s, ur_s, ns_s, nr_s,
):
    rep = lax.axis_index("rep")
    x = lax.axis_index("shard")
    c = lax.rem(rep, CORES)
    zy = lax.div(rep, CORES)
    half = CORES * rpc
    core_dev = (zy * CORES + 1 - c, x)
    x_dev = (rep, 1 - x)
    tiles = pr // RT

    def peer(j):
        return lax.rem(zy + j, zy_n)

    def zy_dev(q):
        return (q * CORES + c, x)

    def piece(k):
        return lax.rem(zy + 1 + k, np_n)

    def rcopy(src, dst, s, r, dev):
        return pltpu.make_async_remote_copy(
            src_ref=src, dst_ref=dst, send_sem=s, recv_sem=r, device_id=dev, device_id_type=MESH
        )

    inner = lax.rem(zy, 2)
    outer = lax.div(zy, 2)
    outer_n = zy_n // 2

    def grads_copy(i, xh, core):
        row = pl.ds(pl.multiple_of(xh * half + core * rpc, RT), rpc)
        return pltpu.make_async_copy(gq_hbm.at[:, row, :], gq.at[:, row, :], in_sem.at[i])

    keys_in = pltpu.make_async_copy(gk_hbm, gk, in_sem.at[4])
    grads_in = [
        grads_copy(0, 0, 1 - c),
        grads_copy(1, 1, 1 - c),
        grads_copy(2, 1 - x, c),
        grads_copy(3, x, c),
    ]
    keys_in.start()
    for one in grads_in:
        one.start()
    states = [(mq_hbm, mq), (oq_hbm, oq), (sq_hbm, sq), (mk_hbm, mkt), (ok_hbm, okt), (sk_hbm, skt)]
    mine = pl.ds(pl.multiple_of(c * rpc, RT), rpc)
    states_in = [
        pltpu.make_async_copy(src.at[mine, :] if i < 3 else src, dst, st_sem.at[i])
        for i, (src, dst) in enumerate(states)
    ]

    barrier = pltpu.get_barrier_semaphore()
    pl.semaphore_signal(barrier, inc=1, device_id=core_dev, device_id_type=MESH)
    pl.semaphore_signal(barrier, inc=1, device_id=x_dev, device_id_type=MESH)

    @pl.loop(1, zy_n)
    def _(j):
        pl.semaphore_signal(barrier, inc=1, device_id=zy_dev(peer(j)), device_id_type=MESH)

    keys_in.wait()
    for lane in range(0, gk.shape[2], 128):
        lanes = slice(lane, min(lane + 128, gk.shape[2]))
        k = gk[0, :, lanes].astype(F32)
        for m in range(1, gk.shape[0]):
            k = k + gk[m, :, lanes].astype(F32)
        lk[lanes, :] = k.T
    grads_in[0].wait()
    grads_in[1].wait()
    pl.semaphore_wait(barrier, zy_n + 1)

    def rows_of(p, t):
        return jnp.minimum(p * pr + t * RT, rpc - RT)

    def lsum(xh, core, p, t):
        row = pl.ds(pl.multiple_of(xh * half + core * rpc + rows_of(p, t), RT), RT)
        q = gq[0, row, :].astype(F32)
        for m in range(1, gq.shape[0]):
            q = q + gq[m, row, :].astype(F32)
        return join(q, lk[row, :])

    def tile(t):
        return pl.ds(t * RT, RT)

    def core_copy(k):
        return rcopy(cs.at[k], cr.at[k], cs_s.at[k], cr_s.at[k], core_dev)

    def x_copy(k):
        return rcopy(xs.at[k], xr.at[k], xs_s.at[k], xr_s.at[k], x_dev)

    def zy_copy(k):
        return rcopy(zs.at[k], zr.at[zy], zs_s.at[k], zr_s.at[zy], zy_dev(piece(k)))

    def zy_arrival(s):
        return rcopy(zs.at[0], zr.at[s], zs_s.at[0], zr_s.at[s], zy_dev(s))

    @pl.loop(0, np_n)
    def _(k):
        p = piece(k)
        for xh in range(2):
            for t in range(tiles):
                cs[k, xh, tile(t), :] = lsum(xh, 1 - c, p, t).astype(BF16)
        core_copy(k).start()

    for one in states_in:
        one.start()
    grads_in[2].wait()
    grads_in[3].wait()

    @pl.loop(0, np_n)
    def _(k):
        p = piece(k)
        core_copy(k).wait_recv()
        for t in range(tiles):
            part = lsum(1 - x, c, p, t) + cr[k, 1 - x, tile(t), :].astype(F32)
            xs[k, tile(t), :] = part.astype(BF16)
        x_copy(k).start()

    for i, (src, dst) in enumerate([(mkt, mk), (okt, ok), (skt, sk)]):
        states_in[3 + i].wait()
        dst[...] = src[...].T

    @pl.loop(0, np_n)
    def _(k):
        p = piece(k)
        x_copy(k).wait_recv()
        for t in range(tiles):
            part = lsum(x, c, p, t) + cr[k, x, tile(t), :].astype(F32)
            part = part + xr[k, tile(t), :].astype(F32)

            @pl.when(p == zy)
            def _():
                own[tile(t), :] = part

            @pl.when(p != zy)
            def _():
                zs[k, tile(t), :] = part.astype(BF16)

        @pl.when(p != zy)
        def _():
            zy_copy(k).start()

    def fold(a):
        total = jnp.zeros((8, 128), F32)
        for r in range(0, a.shape[0], 8):
            for l in range(0, a.shape[1], 128):
                total = total + a[r : r + 8, l : l + 128]
        return total

    def gather_copy(j):
        to = lax.rem(outer + j, outer_n) * 2 + inner
        return rcopy(g.at[c, zy], g.at[c, zy], ags_s.at[j], agr_s.at[zy], zy_dev(to))

    def inner_copy(p):
        return rcopy(g.at[c, p], g.at[c, p], is_s.at[p], agr_s.at[p], zy_dev(zy + 1 - 2 * inner))

    def gather_arrival(p):
        return rcopy(g.at[c, p], g.at[c, p], ags_s.at[0], agr_s.at[p], zy_dev(p))

    def forward(core, p):
        return rcopy(g.at[core, p], g.at[core, p], fs_s.at[p], fr_s.at[p], core_dev)

    norm[0] = jnp.zeros((8, 128), F32)

    @pl.when(zy < np_n)
    def _():
        @pl.loop(1, zy_n)
        def _(j):
            zy_arrival(lax.rem(zy + zy_n - j, zy_n)).wait_recv()

        total = jnp.zeros((8, 128), F32)
        for t in range(tiles):

            def add(j, acc):
                return acc + zr[peer(j), tile(t), :].astype(F32)

            acc = lax.fori_loop(1, zy_n, add, own[tile(t), :])
            g[c, zy, tile(t), :] = acc.astype(BF16)
            valid = (zy * pr + t * RT < rpc).astype(F32)
            total = total + fold(acc * acc) * valid
        norm[0] = total

    def norm_out(j):
        return rcopy(norm.at[0], normx.at[2 + zy], ns_s.at[2 + j], nr_s.at[2 + zy], zy_dev(peer(j)))

    def norm_in(q):
        return rcopy(norm.at[0], normx.at[2 + q], ns_s.at[2], nr_s.at[2 + q], zy_dev(q))

    @pl.loop(1, zy_n)
    def _(j):
        norm_out(j).start()

    @pl.when(zy < np_n)
    def _():
        @pl.loop(1, outer_n)
        def _(j):
            gather_copy(j).start()

        inner_copy(zy).start()

    normx[2 + zy] = norm[0]

    @pl.loop(1, zy_n)
    def _(j):
        norm_in(peer(j)).wait_recv()

    norm[1] = lax.fori_loop(0, zy_n, lambda q, acc: acc + normx[2 + q], jnp.zeros((8, 128), F32))
    norm_first = rcopy(norm.at[1], normx.at[0], ns_s.at[0], nr_s.at[0], core_dev)
    norm_first.start()

    @pl.when(zy < np_n)
    def _():
        forward(c, zy).start()

    norm_first.wait_recv()
    norm[2] = norm[1] + normx[0]
    norm_last = rcopy(norm.at[2], normx.at[1], ns_s.at[1], nr_s.at[1], x_dev)
    norm_last.start()
    norm_last.wait_recv()
    total = norm[2] + normx[1]
    total = jnp.sum(jnp.sum(total, axis=1, keepdims=True), axis=0, keepdims=True)
    limit = jnp.sqrt(jnp.full((1, 1), D * D + D * KV, F32))
    clip = jnp.minimum(1.0, limit / (jnp.sqrt(total) + 1e-06))

    clip_ref[...] = jnp.broadcast_to(clip, (8, 128))
    for one in states_in[:3]:
        one.wait()

    def weights_over(p):
        return rcopy(w.at[x, c, p], w.at[x, c, p], ws_s.at[p], wr_s.at[p], x_dev)

    def weights_in(p):
        return rcopy(w.at[1 - x, c, p], w.at[1 - x, c, p], ws_s.at[p], wr_s.at[p], x_dev)

    def weights_forward(p):
        return rcopy(w.at[1 - x, c, p], w.at[1 - x, c, p], vs_s.at[p], vr_s.at[p], core_dev)

    def weights_last(p):
        return rcopy(w.at[1 - x, 1 - c, p], w.at[1 - x, 1 - c, p], vs_s.at[p], vr_s.at[p], core_dev)

    def weights_near(p):
        return rcopy(w.at[x, c, p], w.at[x, c, p], us_s.at[p], ur_s.at[p], core_dev)

    def weights_near_in(p):
        return rcopy(w.at[x, 1 - c, p], w.at[x, 1 - c, p], us_s.at[p], ur_s.at[p], core_dev)

    def use(p):
        for t in range(tiles):
            row = pl.ds(pl.multiple_of(rows_of(p, t), RT), RT)
            key_row = pl.ds(pl.multiple_of(c * rpc + rows_of(p, t), RT), RT)
            gsq, gsk = split(g[c, p, tile(t), :].astype(F32))
            new_q = adamw(gsq, mq[row, :], oq[row, :], sq[row, :], clip)[0]
            new_k = adamw(gsk, mk[key_row, :], ok[key_row, :], sk[key_row, :], clip)[0]
            w[x, c, p, tile(t), :] = join(new_q, new_k).astype(BF16)
        weights_over(p).start()
        weights_near(p).start()

    @pl.when(zy < np_n)
    def _():
        use(zy)

    @pl.loop(1, outer_n)
    def _(j):
        p = lax.rem(outer + outer_n - j, outer_n) * 2 + inner

        @pl.when(p < np_n)
        def _():
            gather_arrival(p).wait_recv()
            inner_copy(p).start()
            forward(c, p).start()
            use(p)

    @pl.loop(0, outer_n)
    def _(j):
        p = lax.rem(outer + outer_n - j, outer_n) * 2 + 1 - inner

        @pl.when(p < np_n)
        def _():
            gather_arrival(p).wait_recv()
            forward(c, p).start()
            use(p)

    w_own = pltpu.make_async_copy(w.at[x, c], w_hbm.at[x, c], w_sem.at[0])
    w_own.start()

    @pl.loop(0, np_n)
    def _(p):
        forward(1 - c, p).wait_recv()

    g_out = pltpu.make_async_copy(g, g_hbm, w_sem.at[3])
    g_out.start()

    @pl.loop(0, np_n)
    def _(p):
        weights_near_in(p).wait_recv()

    w_near = pltpu.make_async_copy(w.at[x, 1 - c], w_hbm.at[x, 1 - c], w_sem.at[4])
    w_near.start()

    @pl.loop(0, np_n)
    def _(k):
        p = lax.rem(zy + np_n - k, np_n)
        weights_in(p).wait_recv()
        weights_forward(p).start()

    w_c = pltpu.make_async_copy(w.at[1 - x, c], w_hbm.at[1 - x, c], w_sem.at[1])
    w_c.start()

    @pl.loop(0, np_n)
    def _(k):
        weights_last(lax.rem(zy + np_n - k, np_n)).wait_recv()

    w_o = pltpu.make_async_copy(w.at[1 - x, 1 - c], w_hbm.at[1 - x, 1 - c], w_sem.at[2])
    w_o.start()

    @pl.loop(0, np_n)
    def _(k):
        core_copy(k).wait_send()
        x_copy(k).wait_send()

        @pl.when(piece(k) != zy)
        def _():
            zy_copy(k).wait_send()

        forward(c, k).wait_send()
        weights_over(k).wait_send()
        weights_forward(k).wait_send()
        weights_near(k).wait_send()

        @pl.when(lax.rem(k, 2) == inner)
        def _():
            inner_copy(k).wait_send()

    @pl.when(zy < np_n)
    def _():
        @pl.loop(1, outer_n)
        def _(j):
            gather_copy(j).wait_send()

    @pl.loop(1, zy_n)
    def _(j):
        norm_out(j).wait_send()

    norm_first.wait_send()
    norm_last.wait_send()
    for one in [w_own, w_near, g_out, w_c, w_o]:
        one.wait()


def finish(
    np_n, pr, rpc,
    mq_hbm, oq_hbm, sq_hbm, mk_hbm, ok_hbm, sk_hbm, g_hbm, w_hbm, clip_ref,
    nmq_hbm, noq_hbm, nsq_hbm, nmk_hbm, nok_hbm, nsk_hbm, wq_hbm, wk_hbm,
    mq, oq, sq, mk, ok, sk, g, w, wq, wk, wk_rows, gk_rows, gk,
    in_sem, out_sem, more_sem, end_sem,
):
    tiles_all = rpc // RT
    tiles = pr // RT
    parts = 3 if tiles_all % 3 == 0 else 1
    step = tiles_all // parts
    half = CORES * rpc
    clip = clip_ref[0:1, 0:1]

    def block(n):
        return slice(n * step * RT, (n + 1) * step * RT)

    def q_in(n):
        return [
            pltpu.make_async_copy(src.at[block(n), :], dst.at[block(n), :], in_sem.at[n, i])
            for i, (src, dst) in enumerate([(mq_hbm, mq), (oq_hbm, oq), (sq_hbm, sq)])
        ]

    def q_out(n):
        return [
            pltpu.make_async_copy(src.at[block(n), :], dst.at[block(n), :], out_sem.at[n, i])
            for i, (src, dst) in enumerate([(mq, nmq_hbm), (oq, noq_hbm), (sq, nsq_hbm)])
        ]

    g_in = [pltpu.make_async_copy(g_hbm.at[a], g.at[a], more_sem.at[a]) for a in range(CORES)]
    w_in = [pltpu.make_async_copy(w_hbm.at[a], w.at[a], more_sem.at[CORES + a]) for a in range(2)]
    k_in = [
        pltpu.make_async_copy(src, dst, more_sem.at[CORES + 2 + i])
        for i, (src, dst) in enumerate([(mk_hbm, mk), (ok_hbm, ok), (sk_hbm, sk)])
    ]
    total = CORES * parts
    w_in[0].start()
    g_in[0].start()
    for n in range(total):
        for one in q_in(n):
            one.start()
        if n == 0:
            for one in w_in[1:] + g_in[1:]:
                one.start()
    for one in k_in:
        one.start()
    ends = []

    def end(i, src, dst):
        one = pltpu.make_async_copy(src, dst, end_sem.at[i])
        one.start()
        ends.append(one)

    def weights(xh):
        w_in[xh].wait()
        for core in range(CORES):

            @pl.loop(0, tiles_all)
            def _(i):
                row = pl.ds(pl.multiple_of(xh * half + core * rpc + i * RT, RT), RT)
                at = pl.ds(pl.multiple_of(lax.rem(i, tiles) * RT, RT), RT)
                q, k = split(w[xh, core, lax.div(i, tiles), at, :].astype(F32))
                wq[row, :] = q.astype(BF16)
                wk_rows[row, :] = k

        both = slice(xh * half, (xh + 1) * half)
        end(xh, wq.at[both, :], wq_hbm.at[both, :])

    def update(n):
        core = n // parts
        if n % parts == 0:
            g_in[core].wait()
        for one in q_in(n):
            one.wait()

        @pl.loop(n % parts * step, (n % parts + 1) * step)
        def _(i):
            row = pl.ds(pl.multiple_of(core * rpc + i * RT, RT), RT)
            at = pl.ds(pl.multiple_of(lax.rem(i, tiles) * RT, RT), RT)
            gsq, gsk = split(g[core, lax.div(i, tiles), at, :].astype(F32))
            mq[row, :], oq[row, :], sq[row, :] = adamw(gsq, mq[row, :], oq[row, :], sq[row, :], clip)
            gk_rows[row, :] = gsk

        for one in q_out(n):
            one.start()

    weights(0)
    update(0)
    weights(1)
    for n in range(1, total):
        update(n)
    for lane in range(0, wk.shape[1], 128):
        lanes = slice(lane, min(lane + 128, wk.shape[1]))
        wk[:, lanes] = wk_rows[lanes, :].T.astype(BF16)
    end(2, wk, wk_hbm)
    gk[...] = gk_rows[...].T
    for one in k_in:
        one.wait()

    @pl.loop(0, gk.shape[0] // RT)
    def _(i):
        row = pl.ds(pl.multiple_of(i * RT, RT), RT)
        mk[row, :], ok[row, :], sk[row, :] = adamw(gk[row, :], mk[row, :], ok[row, :], sk[row, :], clip)

    for i, (src, dst) in enumerate([(mk, nmk_hbm), (ok, nok_hbm), (sk, nsk_hbm)]):
        end(3 + i, src, dst)
    for n in range(total):
        for one in q_out(n):
            one.wait()
    for one in ends:
        one.wait()


def local(zy_n, grads_query, master_query, moment_query, second_query, grads_keys, master_keys, moment_keys, second_keys):
    half = master_query.shape[0]
    rpc = half // CORES
    tiles_all = rpc // RT
    per = -(-tiles_all // zy_n)
    np_n = -(-tiles_all // per)
    pr = per * RT
    keys = [master_keys, moment_keys, second_keys]
    states = [master_query, moment_query, second_query] + [a.T for a in keys]
    grads_keys = grads_keys.transpose(0, 2, 1)
    sem = lambda n: pltpu.SemaphoreType.DMA((n,))
    any_spec = pl.BlockSpec(memory_space=pl.ANY)
    sums, weights, clip = pl.pallas_call(
        functools.partial(kernel, zy_n, np_n, pr, rpc),
        out_shape=[
            jax.ShapeDtypeStruct((CORES, np_n, pr, WIDE), BF16),
            jax.ShapeDtypeStruct((2, CORES, np_n, pr, WIDE), BF16),
            jax.ShapeDtypeStruct((8, 128), F32),
        ],
        in_specs=[any_spec] * 8,
        out_specs=[any_spec, any_spec, pl.BlockSpec(memory_space=pltpu.VMEM)],
        scratch_shapes=[
            pltpu.VMEM(grads_query.shape, BF16),
            pltpu.VMEM(grads_keys.shape, BF16),
        ]
        + [pltpu.VMEM((rpc, D), F32)] * 3
        + [pltpu.VMEM(a.shape, F32) for a in states[3:] + keys]
        + [pltpu.VMEM((grads_keys.shape[2], grads_keys.shape[1]), F32)]
        + [
            pltpu.VMEM((np_n, 2, pr, WIDE), BF16),
            pltpu.VMEM((np_n, 2, pr, WIDE), BF16),
            pltpu.VMEM((np_n, pr, WIDE), BF16),
            pltpu.VMEM((np_n, pr, WIDE), BF16),
            pltpu.VMEM((np_n, pr, WIDE), BF16),
            pltpu.VMEM((zy_n, pr, WIDE), BF16),
            pltpu.VMEM((pr, WIDE), F32),
            pltpu.VMEM((CORES, np_n, pr, WIDE), BF16),
            pltpu.VMEM((2, CORES, np_n, pr, WIDE), BF16),
            pltpu.VMEM((3, 8, 128), F32),
            pltpu.VMEM((2 + zy_n, 8, 128), F32),
            sem(5), sem(6), sem(5),
            sem(np_n), sem(np_n), sem(np_n), sem(np_n), sem(np_n), sem(zy_n),
            sem(zy_n), sem(np_n), sem(np_n), sem(np_n), sem(np_n),
            sem(np_n), sem(np_n), sem(np_n), sem(np_n), sem(np_n), sem(np_n), sem(2 + zy_n), sem(2 + zy_n),
        ],
        compiler_params=pltpu.CompilerParams(
            collective_id=0, has_side_effects=True, vmem_limit_bytes=56 << 20
        ),
    )(grads_query, *states[:3], grads_keys, *states[3:])
    parts = 3 if tiles_all % 3 == 0 else 1
    outs = pl.pallas_call(
        functools.partial(finish, np_n, pr, rpc),
        out_shape=[jax.ShapeDtypeStruct(a.shape, F32) for a in states]
        + [jax.ShapeDtypeStruct((2 * half, D), BF16), jax.ShapeDtypeStruct((KV, 2 * half), BF16)],
        in_specs=[any_spec] * 8 + [pl.BlockSpec(memory_space=pltpu.VMEM)],
        out_specs=[any_spec] * 8,
        scratch_shapes=[pltpu.VMEM(a.shape, F32) for a in states]
        + [
            pltpu.VMEM(sums.shape, BF16),
            pltpu.VMEM(weights.shape, BF16),
            pltpu.VMEM((2 * half, D), BF16),
            pltpu.VMEM((KV, 2 * half), BF16),
            pltpu.VMEM((2 * half, KV), F32),
            pltpu.VMEM((half, KV), F32),
            pltpu.VMEM((KV, half), F32),
            pltpu.SemaphoreType.DMA((CORES * parts, 3)),
            pltpu.SemaphoreType.DMA((CORES * parts, 3)),
            sem(CORES + 5), sem(6),
        ],
        compiler_params=pltpu.CompilerParams(vmem_limit_bytes=56 << 20),
    )(*states, sums, weights, clip)
    return (*outs[:3], outs[6], *[a.T for a in outs[3:6]], outs[7].T)


def solution(mesh):
    zy_n = mesh.shape["rep"] // CORES
    rows = P("shard", None)
    grads = P(("rep", "shard"), None, None)
    in_specs = (grads, rows, rows, rows, grads, rows, rows, rows)
    out_specs = (rows, rows, rows, P(), rows, rows, rows, P())
    return jax.shard_map(
        functools.partial(local, zy_n), mesh=mesh, in_specs=in_specs, out_specs=out_specs, check_vma=False
    )
```

```python
import functools

import jax
import jax.numpy as jnp
from jax import lax
from jax.experimental import pallas as pl
from jax.experimental.pallas import tpu as pltpu
from jax.sharding import PartitionSpec as P

D = 960
KV = 320
STEP = 10
CORES = 2
RT = 16
WIDE = D + KV
MAIN = KV // 128 * 128
MESH = pl.DeviceIdType.MESH
F32 = jnp.float32
BF16 = jnp.bfloat16


def join(q, k):
    return jnp.concatenate([q, k[:, MAIN:], k[:, :MAIN]], axis=1)


def split(wide):
    rest = KV - MAIN
    return wide[:, :D], jnp.concatenate([wide[:, D + rest :], wide[:, D : D + rest]], axis=1)


def adamw(grad_sum, master, moment, second, clip):
    grad = clip * grad_sum
    new_moment = 0.9 * moment + 0.1 * grad
    new_second = 0.999 * second + 0.001 * grad * grad
    mhat = new_moment * (1.0 / (1.0 - 0.9**STEP))
    vhat = new_second * (1.0 / (1.0 - 0.999**STEP))
    new_master = master - 0.02 * (mhat / (jnp.sqrt(vhat) + 1e-08) + 0.1 * master)
    return new_master, new_moment, new_second


def kernel(
    zy_n, np_n, pr, rpc,
    gq_hbm, mq_hbm, oq_hbm, sq_hbm, gk_hbm, mk_hbm, ok_hbm, sk_hbm,
    g_hbm, w_hbm, clip_ref,
    gq, gk, mq, oq, sq, mkt, okt, skt, mk, ok, sk, lk,
    cs, cr, xs, xr, zs, zr, own, g, w, norm, normx,
    in_sem, st_sem, w_sem,
    cs_s, cr_s, xs_s, xr_s, zs_s, zr_s,
    ags_s, agr_s, is_s, fs_s, fr_s, ws_s, wr_s, ys_s, vs_s, vr_s, us_s, ur_s, ns_s, nr_s,
):
    rep = lax.axis_index("rep")
    x = lax.axis_index("shard")
    c = lax.rem(rep, CORES)
    zy = lax.div(rep, CORES)
    half = CORES * rpc
    core_dev = (zy * CORES + 1 - c, x)
    x_dev = (rep, 1 - x)
    tiles = pr // RT

    def peer(j):
        return lax.rem(zy + j, zy_n)

    def zy_dev(q):
        return (q * CORES + c, x)

    def piece(k):
        return lax.rem(zy + 1 + k, np_n)

    def rcopy(src, dst, s, r, dev):
        return pltpu.make_async_remote_copy(
            src_ref=src, dst_ref=dst, send_sem=s, recv_sem=r, device_id=dev, device_id_type=MESH
        )

    inner = lax.rem(zy, 2)
    outer = lax.div(zy, 2)
    outer_n = zy_n // 2

    def grads_copy(i, xh, core):
        row = pl.ds(pl.multiple_of(xh * half + core * rpc, RT), rpc)
        return pltpu.make_async_copy(gq_hbm.at[:, row, :], gq.at[:, row, :], in_sem.at[i])

    keys_in = pltpu.make_async_copy(gk_hbm, gk, in_sem.at[4])
    grads_in = [
        grads_copy(0, 0, 1 - c),
        grads_copy(1, 1, 1 - c),
        grads_copy(2, 1 - x, c),
        grads_copy(3, x, c),
    ]
    keys_in.start()
    for one in grads_in:
        one.start()
    states = [(mq_hbm, mq), (oq_hbm, oq), (sq_hbm, sq), (mk_hbm, mkt), (ok_hbm, okt), (sk_hbm, skt)]
    mine = pl.ds(pl.multiple_of(c * rpc, RT), rpc)
    states_in = [
        pltpu.make_async_copy(src.at[mine, :] if i < 3 else src, dst, st_sem.at[i])
        for i, (src, dst) in enumerate(states)
    ]

    barrier = pltpu.get_barrier_semaphore()
    pl.semaphore_signal(barrier, inc=1, device_id=core_dev, device_id_type=MESH)
    pl.semaphore_signal(barrier, inc=1, device_id=x_dev, device_id_type=MESH)

    @pl.loop(1, zy_n)
    def _(j):
        pl.semaphore_signal(barrier, inc=1, device_id=zy_dev(peer(j)), device_id_type=MESH)

    keys_in.wait()
    for lane in range(0, gk.shape[2], 128):
        lanes = slice(lane, min(lane + 128, gk.shape[2]))
        k = gk[0, :, lanes].astype(F32)
        for m in range(1, gk.shape[0]):
            k = k + gk[m, :, lanes].astype(F32)
        lk[lanes, :] = k.T
    grads_in[0].wait()
    grads_in[1].wait()
    pl.semaphore_wait(barrier, zy_n + 1)

    def rows_of(p, t):
        return jnp.minimum(p * pr + t * RT, rpc - RT)

    def lsum(xh, core, p, t):
        row = pl.ds(pl.multiple_of(xh * half + core * rpc + rows_of(p, t), RT), RT)
        q = gq[0, row, :].astype(F32)
        for m in range(1, gq.shape[0]):
            q = q + gq[m, row, :].astype(F32)
        return join(q, lk[row, :])

    def tile(t):
        return pl.ds(t * RT, RT)

    def core_copy(k):
        return rcopy(cs.at[k], cr.at[k], cs_s.at[k], cr_s.at[k], core_dev)

    def x_copy(k):
        return rcopy(xs.at[k], xr.at[k], xs_s.at[k], xr_s.at[k], x_dev)

    def zy_copy(k):
        return rcopy(zs.at[k], zr.at[zy], zs_s.at[k], zr_s.at[zy], zy_dev(piece(k)))

    def zy_arrival(s):
        return rcopy(zs.at[0], zr.at[s], zs_s.at[0], zr_s.at[s], zy_dev(s))

    @pl.loop(0, np_n)
    def _(k):
        p = piece(k)
        for xh in range(2):
            for t in range(tiles):
                cs[k, xh, tile(t), :] = lsum(xh, 1 - c, p, t).astype(BF16)
        core_copy(k).start()

    for one in states_in:
        one.start()
    grads_in[2].wait()
    grads_in[3].wait()

    @pl.loop(0, np_n)
    def _(k):
        p = piece(k)
        core_copy(k).wait_recv()
        for t in range(tiles):
            part = lsum(1 - x, c, p, t) + cr[k, 1 - x, tile(t), :].astype(F32)
            xs[k, tile(t), :] = part.astype(BF16)
        x_copy(k).start()

    for i, (src, dst) in enumerate([(mkt, mk), (okt, ok), (skt, sk)]):
        states_in[3 + i].wait()
        dst[...] = src[...].T

    @pl.loop(0, np_n)
    def _(k):
        p = piece(k)
        x_copy(k).wait_recv()
        for t in range(tiles):
            part = lsum(x, c, p, t) + cr[k, x, tile(t), :].astype(F32)
            part = part + xr[k, tile(t), :].astype(F32)

            @pl.when(p == zy)
            def _():
                own[tile(t), :] = part

            @pl.when(p != zy)
            def _():
                zs[k, tile(t), :] = part.astype(BF16)

        @pl.when(p != zy)
        def _():
            zy_copy(k).start()

    def fold(a):
        total = jnp.zeros((8, 128), F32)
        for r in range(0, a.shape[0], 8):
            for l in range(0, a.shape[1], 128):
                total = total + a[r : r + 8, l : l + 128]
        return total

    def gather_copy(j):
        to = lax.rem(outer + j, outer_n) * 2 + inner
        return rcopy(g.at[c, zy], g.at[c, zy], ags_s.at[j], agr_s.at[zy], zy_dev(to))

    def inner_copy(p):
        return rcopy(g.at[c, p], g.at[c, p], is_s.at[p], agr_s.at[p], zy_dev(zy + 1 - 2 * inner))

    def gather_arrival(p):
        return rcopy(g.at[c, p], g.at[c, p], ags_s.at[0], agr_s.at[p], zy_dev(p))

    def forward(core, p):
        return rcopy(g.at[core, p], g.at[core, p], fs_s.at[p], fr_s.at[p], core_dev)

    norm[0] = jnp.zeros((8, 128), F32)

    @pl.when(zy < np_n)
    def _():
        @pl.loop(1, zy_n)
        def _(j):
            zy_arrival(lax.rem(zy + zy_n - j, zy_n)).wait_recv()

        total = jnp.zeros((8, 128), F32)
        for t in range(tiles):

            def add(j, acc):
                return acc + zr[peer(j), tile(t), :].astype(F32)

            acc = lax.fori_loop(1, zy_n, add, own[tile(t), :])
            g[c, zy, tile(t), :] = acc.astype(BF16)
            valid = (zy * pr + t * RT < rpc).astype(F32)
            total = total + fold(acc * acc) * valid
        norm[0] = total

    def norm_out(j):
        return rcopy(norm.at[0], normx.at[2 + zy], ns_s.at[2 + j], nr_s.at[2 + zy], zy_dev(peer(j)))

    def norm_in(q):
        return rcopy(norm.at[0], normx.at[2 + q], ns_s.at[2], nr_s.at[2 + q], zy_dev(q))

    @pl.loop(1, zy_n)
    def _(j):
        norm_out(j).start()

    @pl.when(zy < np_n)
    def _():
        @pl.loop(1, outer_n)
        def _(j):
            gather_copy(j).start()

        inner_copy(zy).start()

    normx[2 + zy] = norm[0]

    @pl.loop(1, zy_n)
    def _(j):
        norm_in(peer(j)).wait_recv()

    norm[1] = lax.fori_loop(0, zy_n, lambda q, acc: acc + normx[2 + q], jnp.zeros((8, 128), F32))
    norm_first = rcopy(norm.at[1], normx.at[0], ns_s.at[0], nr_s.at[0], core_dev)
    norm_first.start()

    @pl.when(zy < np_n)
    def _():
        forward(c, zy).start()

    norm_first.wait_recv()
    norm[2] = norm[1] + normx[0]
    norm_last = rcopy(norm.at[2], normx.at[1], ns_s.at[1], nr_s.at[1], x_dev)
    norm_last.start()
    norm_last.wait_recv()
    total = norm[2] + normx[1]
    total = jnp.sum(jnp.sum(total, axis=1, keepdims=True), axis=0, keepdims=True)
    limit = jnp.sqrt(jnp.full((1, 1), D * D + D * KV, F32))
    clip = jnp.minimum(1.0, limit / (jnp.sqrt(total) + 1e-06))

    clip_ref[...] = jnp.broadcast_to(clip, (8, 128))
    for one in states_in[:3]:
        one.wait()

    def weights_over(p):
        return rcopy(w.at[x, c, p], w.at[x, c, p], ws_s.at[p], wr_s.at[p], x_dev)

    def weights_in(p):
        return rcopy(w.at[1 - x, c, p], w.at[1 - x, c, p], ws_s.at[p], wr_s.at[p], x_dev)

    def weights_inner(p):
        return rcopy(w.at[1 - x, c, p], w.at[1 - x, c, p], ys_s.at[p], wr_s.at[p], zy_dev(zy + 1 - 2 * inner))

    def weights_forward(p):
        return rcopy(w.at[1 - x, c, p], w.at[1 - x, c, p], vs_s.at[p], vr_s.at[p], core_dev)

    def weights_last(p):
        return rcopy(w.at[1 - x, 1 - c, p], w.at[1 - x, 1 - c, p], vs_s.at[p], vr_s.at[p], core_dev)

    def weights_near(p):
        return rcopy(w.at[x, c, p], w.at[x, c, p], us_s.at[p], ur_s.at[p], core_dev)

    def weights_near_in(p):
        return rcopy(w.at[x, 1 - c, p], w.at[x, 1 - c, p], us_s.at[p], ur_s.at[p], core_dev)

    def use(p):
        for t in range(tiles):
            row = pl.ds(pl.multiple_of(rows_of(p, t), RT), RT)
            key_row = pl.ds(pl.multiple_of(c * rpc + rows_of(p, t), RT), RT)
            gsq, gsk = split(g[c, p, tile(t), :].astype(F32))
            new_q = adamw(gsq, mq[row, :], oq[row, :], sq[row, :], clip)[0]
            new_k = adamw(gsk, mk[key_row, :], ok[key_row, :], sk[key_row, :], clip)[0]
            w[x, c, p, tile(t), :] = join(new_q, new_k).astype(BF16)
        weights_near(p).start()

    @pl.when(zy < np_n)
    def _():
        use(zy)
        weights_over(zy).start()

    @pl.loop(1, outer_n)
    def _(j):
        p = lax.rem(outer + outer_n - j, outer_n) * 2 + inner

        @pl.when(p < np_n)
        def _():
            gather_arrival(p).wait_recv()
            inner_copy(p).start()
            forward(c, p).start()
            use(p)
            weights_over(p).start()

    @pl.loop(0, outer_n)
    def _(j):
        p = lax.rem(outer + outer_n - j, outer_n) * 2 + inner

        @pl.when(p < np_n)
        def _():
            weights_in(p).wait_recv()
            weights_inner(p).start()
            weights_forward(p).start()

    @pl.loop(0, outer_n)
    def _(j):
        p = lax.rem(outer + outer_n - j, outer_n) * 2 + 1 - inner

        @pl.when(p < np_n)
        def _():
            gather_arrival(p).wait_recv()
            forward(c, p).start()
            use(p)

    w_own = pltpu.make_async_copy(w.at[x, c], w_hbm.at[x, c], w_sem.at[0])
    w_own.start()

    @pl.loop(0, np_n)
    def _(p):
        forward(1 - c, p).wait_recv()

    g_out = pltpu.make_async_copy(g, g_hbm, w_sem.at[3])
    g_out.start()

    @pl.loop(0, np_n)
    def _(p):
        weights_near_in(p).wait_recv()

    w_near = pltpu.make_async_copy(w.at[x, 1 - c], w_hbm.at[x, 1 - c], w_sem.at[4])
    w_near.start()

    @pl.loop(0, outer_n)
    def _(j):
        p = lax.rem(outer + outer_n - j, outer_n) * 2 + 1 - inner

        @pl.when(p < np_n)
        def _():
            weights_in(p).wait_recv()
            weights_forward(p).start()

    w_c = pltpu.make_async_copy(w.at[1 - x, c], w_hbm.at[1 - x, c], w_sem.at[1])
    w_c.start()

    @pl.loop(0, np_n)
    def _(k):
        weights_last(lax.rem(zy + np_n - k, np_n)).wait_recv()

    w_o = pltpu.make_async_copy(w.at[1 - x, 1 - c], w_hbm.at[1 - x, 1 - c], w_sem.at[2])
    w_o.start()

    @pl.loop(0, np_n)
    def _(k):
        core_copy(k).wait_send()
        x_copy(k).wait_send()

        @pl.when(piece(k) != zy)
        def _():
            zy_copy(k).wait_send()

        forward(c, k).wait_send()
        weights_forward(k).wait_send()
        weights_near(k).wait_send()

        @pl.when(lax.rem(k, 2) == inner)
        def _():
            inner_copy(k).wait_send()
            weights_over(k).wait_send()
            weights_inner(k).wait_send()

    @pl.when(zy < np_n)
    def _():
        @pl.loop(1, outer_n)
        def _(j):
            gather_copy(j).wait_send()

    @pl.loop(1, zy_n)
    def _(j):
        norm_out(j).wait_send()

    norm_first.wait_send()
    norm_last.wait_send()
    for one in [w_own, w_near, g_out, w_c, w_o]:
        one.wait()


def finish(
    np_n, pr, rpc,
    mq_hbm, oq_hbm, sq_hbm, mk_hbm, ok_hbm, sk_hbm, g_hbm, w_hbm, clip_ref,
    nmq_hbm, noq_hbm, nsq_hbm, nmk_hbm, nok_hbm, nsk_hbm, wq_hbm, wk_hbm,
    mq, oq, sq, mk, ok, sk, g, w, wq, wk, wk_rows, gk_rows, gk,
    in_sem, out_sem, more_sem, end_sem,
):
    tiles_all = rpc // RT
    tiles = pr // RT
    parts = 3 if tiles_all % 3 == 0 else 1
    step = tiles_all // parts
    half = CORES * rpc
    clip = clip_ref[0:1, 0:1]

    def block(n):
        return slice(n * step * RT, (n + 1) * step * RT)

    def q_in(n):
        return [
            pltpu.make_async_copy(src.at[block(n), :], dst.at[block(n), :], in_sem.at[n, i])
            for i, (src, dst) in enumerate([(mq_hbm, mq), (oq_hbm, oq), (sq_hbm, sq)])
        ]

    def q_out(n):
        return [
            pltpu.make_async_copy(src.at[block(n), :], dst.at[block(n), :], out_sem.at[n, i])
            for i, (src, dst) in enumerate([(mq, nmq_hbm), (oq, noq_hbm), (sq, nsq_hbm)])
        ]

    g_in = [pltpu.make_async_copy(g_hbm.at[a], g.at[a], more_sem.at[a]) for a in range(CORES)]
    w_in = [pltpu.make_async_copy(w_hbm.at[a], w.at[a], more_sem.at[CORES + a]) for a in range(2)]
    k_in = [
        pltpu.make_async_copy(src, dst, more_sem.at[CORES + 2 + i])
        for i, (src, dst) in enumerate([(mk_hbm, mk), (ok_hbm, ok), (sk_hbm, sk)])
    ]
    total = CORES * parts
    w_in[0].start()
    g_in[0].start()
    for n in range(total):
        for one in q_in(n):
            one.start()
        if n == 0:
            for one in w_in[1:] + g_in[1:]:
                one.start()
    for one in k_in:
        one.start()
    ends = []

    def end(i, src, dst):
        one = pltpu.make_async_copy(src, dst, end_sem.at[i])
        one.start()
        ends.append(one)

    def weights(xh):
        w_in[xh].wait()
        for core in range(CORES):

            @pl.loop(0, tiles_all)
            def _(i):
                row = pl.ds(pl.multiple_of(xh * half + core * rpc + i * RT, RT), RT)
                at = pl.ds(pl.multiple_of(lax.rem(i, tiles) * RT, RT), RT)
                q, k = split(w[xh, core, lax.div(i, tiles), at, :].astype(F32))
                wq[row, :] = q.astype(BF16)
                wk_rows[row, :] = k

        both = slice(xh * half, (xh + 1) * half)
        end(xh, wq.at[both, :], wq_hbm.at[both, :])

    def update(n):
        core = n // parts
        if n % parts == 0:
            g_in[core].wait()
        for one in q_in(n):
            one.wait()

        @pl.loop(n % parts * step, (n % parts + 1) * step)
        def _(i):
            row = pl.ds(pl.multiple_of(core * rpc + i * RT, RT), RT)
            at = pl.ds(pl.multiple_of(lax.rem(i, tiles) * RT, RT), RT)
            gsq, gsk = split(g[core, lax.div(i, tiles), at, :].astype(F32))
            mq[row, :], oq[row, :], sq[row, :] = adamw(gsq, mq[row, :], oq[row, :], sq[row, :], clip)
            gk_rows[row, :] = gsk

        for one in q_out(n):
            one.start()

    weights(0)
    update(0)
    weights(1)
    for lane in range(0, wk.shape[1], 128):
        lanes = slice(lane, min(lane + 128, wk.shape[1]))
        wk[:, lanes] = wk_rows[lanes, :].T.astype(BF16)
    end(2, wk, wk_hbm)
    for n in range(1, total):
        update(n)
    gk[...] = gk_rows[...].T
    for one in k_in:
        one.wait()

    @pl.loop(0, gk.shape[0] // RT)
    def _(i):
        row = pl.ds(pl.multiple_of(i * RT, RT), RT)
        mk[row, :], ok[row, :], sk[row, :] = adamw(gk[row, :], mk[row, :], ok[row, :], sk[row, :], clip)

    for i, (src, dst) in enumerate([(mk, nmk_hbm), (ok, nok_hbm), (sk, nsk_hbm)]):
        end(3 + i, src, dst)
    for n in range(total):
        for one in q_out(n):
            one.wait()
    for one in ends:
        one.wait()


def local(zy_n, grads_query, master_query, moment_query, second_query, grads_keys, master_keys, moment_keys, second_keys):
    half = master_query.shape[0]
    rpc = half // CORES
    tiles_all = rpc // RT
    per = -(-tiles_all // zy_n)
    np_n = -(-tiles_all // per)
    pr = per * RT
    keys = [master_keys, moment_keys, second_keys]
    states = [master_query, moment_query, second_query] + [a.T for a in keys]
    grads_keys = grads_keys.transpose(0, 2, 1)
    sem = lambda n: pltpu.SemaphoreType.DMA((n,))
    any_spec = pl.BlockSpec(memory_space=pl.ANY)
    sums, weights, clip = pl.pallas_call(
        functools.partial(kernel, zy_n, np_n, pr, rpc),
        out_shape=[
            jax.ShapeDtypeStruct((CORES, np_n, pr, WIDE), BF16),
            jax.ShapeDtypeStruct((2, CORES, np_n, pr, WIDE), BF16),
            jax.ShapeDtypeStruct((8, 128), F32),
        ],
        in_specs=[any_spec] * 8,
        out_specs=[any_spec, any_spec, pl.BlockSpec(memory_space=pltpu.VMEM)],
        scratch_shapes=[
            pltpu.VMEM(grads_query.shape, BF16),
            pltpu.VMEM(grads_keys.shape, BF16),
        ]
        + [pltpu.VMEM((rpc, D), F32)] * 3
        + [pltpu.VMEM(a.shape, F32) for a in states[3:] + keys]
        + [pltpu.VMEM((grads_keys.shape[2], grads_keys.shape[1]), F32)]
        + [
            pltpu.VMEM((np_n, 2, pr, WIDE), BF16),
            pltpu.VMEM((np_n, 2, pr, WIDE), BF16),
            pltpu.VMEM((np_n, pr, WIDE), BF16),
            pltpu.VMEM((np_n, pr, WIDE), BF16),
            pltpu.VMEM((np_n, pr, WIDE), BF16),
            pltpu.VMEM((zy_n, pr, WIDE), BF16),
            pltpu.VMEM((pr, WIDE), F32),
            pltpu.VMEM((CORES, np_n, pr, WIDE), BF16),
            pltpu.VMEM((2, CORES, np_n, pr, WIDE), BF16),
            pltpu.VMEM((3, 8, 128), F32),
            pltpu.VMEM((2 + zy_n, 8, 128), F32),
            sem(5), sem(6), sem(5),
            sem(np_n), sem(np_n), sem(np_n), sem(np_n), sem(np_n), sem(zy_n),
            sem(zy_n), sem(np_n), sem(np_n), sem(np_n), sem(np_n),
            sem(np_n), sem(np_n), sem(np_n), sem(np_n), sem(np_n), sem(np_n), sem(np_n), sem(2 + zy_n), sem(2 + zy_n),
        ],
        compiler_params=pltpu.CompilerParams(
            collective_id=0, has_side_effects=True, vmem_limit_bytes=56 << 20
        ),
    )(grads_query, *states[:3], grads_keys, *states[3:])
    parts = 3 if tiles_all % 3 == 0 else 1
    outs = pl.pallas_call(
        functools.partial(finish, np_n, pr, rpc),
        out_shape=[jax.ShapeDtypeStruct(a.shape, F32) for a in states]
        + [jax.ShapeDtypeStruct((2 * half, D), BF16), jax.ShapeDtypeStruct((KV, 2 * half), BF16)],
        in_specs=[any_spec] * 8 + [pl.BlockSpec(memory_space=pltpu.VMEM)],
        out_specs=[any_spec] * 8,
        scratch_shapes=[pltpu.VMEM(a.shape, F32) for a in states]
        + [
            pltpu.VMEM(sums.shape, BF16),
            pltpu.VMEM(weights.shape, BF16),
            pltpu.VMEM((2 * half, D), BF16),
            pltpu.VMEM((KV, 2 * half), BF16),
            pltpu.VMEM((2 * half, KV), F32),
            pltpu.VMEM((half, KV), F32),
            pltpu.VMEM((KV, half), F32),
            pltpu.SemaphoreType.DMA((CORES * parts, 3)),
            pltpu.SemaphoreType.DMA((CORES * parts, 3)),
            sem(CORES + 5), sem(6),
        ],
        compiler_params=pltpu.CompilerParams(vmem_limit_bytes=56 << 20),
    )(*states, sums, weights, clip)
    return (*outs[:3], outs[6], *[a.T for a in outs[3:6]], outs[7].T)


def solution(mesh):
    zy_n = mesh.shape["rep"] // CORES
    rows = P("shard", None)
    grads = P(("rep", "shard"), None, None)
    in_specs = (grads, rows, rows, rows, grads, rows, rows, rows)
    out_specs = (rows, rows, rows, P(), rows, rows, rows, P())
    return jax.shard_map(
        functools.partial(local, zy_n), mesh=mesh, in_specs=in_specs, out_specs=out_specs, check_vma=False
    )
```

```python
import functools

import jax
import jax.numpy as jnp
from jax import lax
from jax.experimental import pallas as pl
from jax.experimental.pallas import tpu as pltpu
from jax.sharding import PartitionSpec as P

D = 960
KV = 320
STEP = 10
CORES = 2
RT = 16
WIDE = D + KV
MAIN = KV // 128 * 128
MESH = pl.DeviceIdType.MESH
F32 = jnp.float32
BF16 = jnp.bfloat16


def join(q, k):
    return jnp.concatenate([q, k[:, MAIN:], k[:, :MAIN]], axis=1)


def split(wide):
    rest = KV - MAIN
    return wide[:, :D], jnp.concatenate([wide[:, D + rest :], wide[:, D : D + rest]], axis=1)


def adamw(grad_sum, master, moment, second, clip):
    grad = clip * grad_sum
    new_moment = 0.9 * moment + 0.1 * grad
    new_second = 0.999 * second + 0.001 * grad * grad
    mhat = new_moment * (1.0 / (1.0 - 0.9**STEP))
    vhat = new_second * (1.0 / (1.0 - 0.999**STEP))
    new_master = master - 0.02 * (mhat / (jnp.sqrt(vhat) + 1e-08) + 0.1 * master)
    return new_master, new_moment, new_second


def kernel(
    zy_n, np_n, pr, rpc,
    gq_hbm, mq_hbm, oq_hbm, sq_hbm, gk_hbm, mk_hbm, ok_hbm, sk_hbm,
    g_hbm, w_hbm, clip_ref,
    gq, gk, mq, oq, sq, mkt, okt, skt, mk, ok, sk, lk,
    cs, cr, xs, xr, zs, zr, own, g, w, norm, normx,
    in_sem, st_sem, w_sem,
    cs_s, cr_s, xs_s, xr_s, zs_s, zr_s,
    ags_s, agr_s, is_s, fs_s, fr_s, ws_s, wr_s, ys_s, vs_s, vr_s, us_s, ur_s, ns_s, nr_s,
):
    rep = lax.axis_index("rep")
    x = lax.axis_index("shard")
    c = lax.rem(rep, CORES)
    zy = lax.div(rep, CORES)
    half = CORES * rpc
    core_dev = (zy * CORES + 1 - c, x)
    x_dev = (rep, 1 - x)
    tiles = pr // RT

    def peer(j):
        return lax.rem(zy + j, zy_n)

    def zy_dev(q):
        return (q * CORES + c, x)

    def piece(k):
        return lax.rem(zy + 1 + k, np_n)

    def rcopy(src, dst, s, r, dev):
        return pltpu.make_async_remote_copy(
            src_ref=src, dst_ref=dst, send_sem=s, recv_sem=r, device_id=dev, device_id_type=MESH
        )

    inner = lax.rem(zy, 2)
    outer = lax.div(zy, 2)
    outer_n = zy_n // 2

    def grads_copy(i, xh, core):
        row = pl.ds(pl.multiple_of(xh * half + core * rpc, RT), rpc)
        return pltpu.make_async_copy(gq_hbm.at[:, row, :], gq.at[:, row, :], in_sem.at[i])

    keys_in = pltpu.make_async_copy(gk_hbm, gk, in_sem.at[4])
    grads_in = [
        grads_copy(0, 0, 1 - c),
        grads_copy(1, 1, 1 - c),
        grads_copy(2, 1 - x, c),
        grads_copy(3, x, c),
    ]
    keys_in.start()
    for one in grads_in:
        one.start()
    states = [(mq_hbm, mq), (oq_hbm, oq), (sq_hbm, sq), (mk_hbm, mkt), (ok_hbm, okt), (sk_hbm, skt)]
    mine = pl.ds(pl.multiple_of(c * rpc, RT), rpc)
    states_in = [
        pltpu.make_async_copy(src.at[mine, :] if i < 3 else src, dst, st_sem.at[i])
        for i, (src, dst) in enumerate(states)
    ]

    barrier = pltpu.get_barrier_semaphore()
    pl.semaphore_signal(barrier, inc=1, device_id=core_dev, device_id_type=MESH)
    pl.semaphore_signal(barrier, inc=1, device_id=x_dev, device_id_type=MESH)

    @pl.loop(1, zy_n)
    def _(j):
        pl.semaphore_signal(barrier, inc=1, device_id=zy_dev(peer(j)), device_id_type=MESH)

    keys_in.wait()
    for lane in range(0, gk.shape[2], 128):
        lanes = slice(lane, min(lane + 128, gk.shape[2]))
        k = gk[0, :, lanes].astype(F32)
        for m in range(1, gk.shape[0]):
            k = k + gk[m, :, lanes].astype(F32)
        lk[lanes, :] = k.T
    grads_in[0].wait()
    grads_in[1].wait()
    pl.semaphore_wait(barrier, zy_n + 1)

    def rows_of(p, t):
        return jnp.minimum(p * pr + t * RT, rpc - RT)

    def lsum(xh, core, p, t):
        row = pl.ds(pl.multiple_of(xh * half + core * rpc + rows_of(p, t), RT), RT)
        q = gq[0, row, :].astype(F32)
        for m in range(1, gq.shape[0]):
            q = q + gq[m, row, :].astype(F32)
        return join(q, lk[row, :])

    def tile(t):
        return pl.ds(t * RT, RT)

    def core_copy(k):
        return rcopy(cs.at[k], cr.at[k], cs_s.at[k], cr_s.at[k], core_dev)

    def x_copy(k):
        return rcopy(xs.at[k], xr.at[k], xs_s.at[k], xr_s.at[k], x_dev)

    def zy_copy(k):
        return rcopy(zs.at[k], zr.at[zy], zs_s.at[k], zr_s.at[zy], zy_dev(piece(k)))

    def zy_arrival(s):
        return rcopy(zs.at[0], zr.at[s], zs_s.at[0], zr_s.at[s], zy_dev(s))

    @pl.loop(0, np_n)
    def _(k):
        p = piece(k)
        for xh in range(2):
            for t in range(tiles):
                cs[k, xh, tile(t), :] = lsum(xh, 1 - c, p, t).astype(BF16)
        core_copy(k).start()

    for one in states_in:
        one.start()
    grads_in[2].wait()
    grads_in[3].wait()

    @pl.loop(0, np_n)
    def _(k):
        p = piece(k)
        core_copy(k).wait_recv()
        for t in range(tiles):
            part = lsum(1 - x, c, p, t) + cr[k, 1 - x, tile(t), :].astype(F32)
            xs[k, tile(t), :] = part.astype(BF16)
        x_copy(k).start()

    for i, (src, dst) in enumerate([(mkt, mk), (okt, ok), (skt, sk)]):
        states_in[3 + i].wait()
        dst[...] = src[...].T

    @pl.loop(0, np_n)
    def _(k):
        p = piece(k)
        x_copy(k).wait_recv()
        for t in range(tiles):
            part = lsum(x, c, p, t) + cr[k, x, tile(t), :].astype(F32)
            part = part + xr[k, tile(t), :].astype(F32)

            @pl.when(p == zy)
            def _():
                own[tile(t), :] = part

            @pl.when(p != zy)
            def _():
                zs[k, tile(t), :] = part.astype(BF16)

        @pl.when(p != zy)
        def _():
            zy_copy(k).start()

    def fold(a):
        total = jnp.zeros((8, 128), F32)
        for r in range(0, a.shape[0], 8):
            for l in range(0, a.shape[1], 128):
                total = total + a[r : r + 8, l : l + 128]
        return total

    def gather_copy(j):
        to = lax.rem(outer + j, outer_n) * 2 + inner
        return rcopy(g.at[c, zy], g.at[c, zy], ags_s.at[j], agr_s.at[zy], zy_dev(to))

    def inner_copy(p):
        return rcopy(g.at[c, p], g.at[c, p], is_s.at[p], agr_s.at[p], zy_dev(zy + 1 - 2 * inner))

    def gather_arrival(p):
        return rcopy(g.at[c, p], g.at[c, p], ags_s.at[0], agr_s.at[p], zy_dev(p))

    def forward(core, p):
        return rcopy(g.at[core, p], g.at[core, p], fs_s.at[p], fr_s.at[p], core_dev)

    norm[0] = jnp.zeros((8, 128), F32)

    @pl.when(zy < np_n)
    def _():
        @pl.loop(1, zy_n)
        def _(j):
            zy_arrival(lax.rem(zy + zy_n - j, zy_n)).wait_recv()

        total = jnp.zeros((8, 128), F32)
        for t in range(tiles):

            def add(j, acc):
                return acc + zr[peer(j), tile(t), :].astype(F32)

            acc = lax.fori_loop(1, zy_n, add, own[tile(t), :])
            g[c, zy, tile(t), :] = acc.astype(BF16)
            valid = (zy * pr + t * RT < rpc).astype(F32)
            total = total + fold(acc * acc) * valid
        norm[0] = total

    def norm_out(j):
        return rcopy(norm.at[0], normx.at[2 + zy], ns_s.at[2 + j], nr_s.at[2 + zy], zy_dev(peer(j)))

    def norm_in(q):
        return rcopy(norm.at[0], normx.at[2 + q], ns_s.at[2], nr_s.at[2 + q], zy_dev(q))

    @pl.loop(1, zy_n)
    def _(j):
        norm_out(j).start()

    @pl.when(zy < np_n)
    def _():
        @pl.loop(1, outer_n)
        def _(j):
            gather_copy(j).start()

        inner_copy(zy).start()

    normx[2 + zy] = norm[0]

    @pl.loop(1, zy_n)
    def _(j):
        norm_in(peer(j)).wait_recv()

    norm[1] = lax.fori_loop(0, zy_n, lambda q, acc: acc + normx[2 + q], jnp.zeros((8, 128), F32))
    norm_first = rcopy(norm.at[1], normx.at[0], ns_s.at[0], nr_s.at[0], core_dev)
    norm_first.start()

    @pl.when(zy < np_n)
    def _():
        forward(c, zy).start()

    norm_first.wait_recv()
    norm[2] = norm[1] + normx[0]
    norm_last = rcopy(norm.at[2], normx.at[1], ns_s.at[1], nr_s.at[1], x_dev)
    norm_last.start()
    norm_last.wait_recv()
    total = norm[2] + normx[1]
    total = jnp.sum(jnp.sum(total, axis=1, keepdims=True), axis=0, keepdims=True)
    limit = jnp.sqrt(jnp.full((1, 1), D * D + D * KV, F32))
    clip = jnp.minimum(1.0, limit / (jnp.sqrt(total) + 1e-06))

    clip_ref[...] = jnp.broadcast_to(clip, (8, 128))
    for one in states_in[:3]:
        one.wait()

    def weights_over(p):
        return rcopy(w.at[x, c, p], w.at[x, c, p], ws_s.at[p], wr_s.at[p], x_dev)

    def weights_in(p):
        return rcopy(w.at[1 - x, c, p], w.at[1 - x, c, p], ws_s.at[p], wr_s.at[p], x_dev)

    def weights_inner(p):
        return rcopy(w.at[1 - x, c, p], w.at[1 - x, c, p], ys_s.at[p], wr_s.at[p], zy_dev(zy + 1 - 2 * inner))

    def weights_forward(p):
        return rcopy(w.at[1 - x, c, p], w.at[1 - x, c, p], vs_s.at[p], vr_s.at[p], core_dev)

    def weights_last(p):
        return rcopy(w.at[1 - x, 1 - c, p], w.at[1 - x, 1 - c, p], vs_s.at[p], vr_s.at[p], core_dev)

    def weights_near(p):
        return rcopy(w.at[x, c, p], w.at[x, c, p], us_s.at[p], ur_s.at[p], core_dev)

    def weights_near_in(p):
        return rcopy(w.at[x, 1 - c, p], w.at[x, 1 - c, p], us_s.at[p], ur_s.at[p], core_dev)

    def use(p):
        for t in range(tiles):
            row = pl.ds(pl.multiple_of(rows_of(p, t), RT), RT)
            key_row = pl.ds(pl.multiple_of(c * rpc + rows_of(p, t), RT), RT)
            gsq, gsk = split(g[c, p, tile(t), :].astype(F32))
            new_q = adamw(gsq, mq[row, :], oq[row, :], sq[row, :], clip)[0]
            new_k = adamw(gsk, mk[key_row, :], ok[key_row, :], sk[key_row, :], clip)[0]
            w[x, c, p, tile(t), :] = join(new_q, new_k).astype(BF16)
        weights_near(p).start()

    @pl.when(zy < np_n)
    def _():
        use(zy)
        weights_over(zy).start()

    @pl.loop(1, outer_n)
    def _(j):
        p = lax.rem(outer + outer_n - j, outer_n) * 2 + inner

        @pl.when(p < np_n)
        def _():
            gather_arrival(p).wait_recv()
            inner_copy(p).start()
            forward(c, p).start()
            use(p)
            weights_over(p).start()

    @pl.loop(0, outer_n)
    def _(j):
        p = lax.rem(outer + outer_n - j, outer_n) * 2 + inner

        @pl.when(p < np_n)
        def _():
            weights_in(p).wait_recv()
            weights_inner(p).start()
            weights_forward(p).start()

    @pl.loop(0, outer_n)
    def _(j):
        p = lax.rem(outer + outer_n - j, outer_n) * 2 + 1 - inner

        @pl.when(p < np_n)
        def _():
            gather_arrival(p).wait_recv()
            forward(c, p).start()
            use(p)

    w_own = pltpu.make_async_copy(w.at[x, c], w_hbm.at[x, c], w_sem.at[0])
    w_own.start()

    @pl.loop(0, np_n)
    def _(p):
        forward(1 - c, p).wait_recv()

    g_out = pltpu.make_async_copy(g, g_hbm, w_sem.at[3])
    g_out.start()

    @pl.loop(0, np_n)
    def _(p):
        weights_near_in(p).wait_recv()

    w_near = pltpu.make_async_copy(w.at[x, 1 - c], w_hbm.at[x, 1 - c], w_sem.at[4])
    w_near.start()

    @pl.loop(0, outer_n)
    def _(j):
        p = lax.rem(outer + outer_n - j, outer_n) * 2 + 1 - inner

        @pl.when(p < np_n)
        def _():
            weights_in(p).wait_recv()
            weights_forward(p).start()

    w_c = pltpu.make_async_copy(w.at[1 - x, c], w_hbm.at[1 - x, c], w_sem.at[1])
    w_c.start()

    @pl.loop(0, np_n)
    def _(k):
        weights_last(lax.rem(zy + np_n - k, np_n)).wait_recv()

    w_o = pltpu.make_async_copy(w.at[1 - x, 1 - c], w_hbm.at[1 - x, 1 - c], w_sem.at[2])
    w_o.start()

    @pl.loop(0, np_n)
    def _(k):
        core_copy(k).wait_send()
        x_copy(k).wait_send()

        @pl.when(piece(k) != zy)
        def _():
            zy_copy(k).wait_send()

        forward(c, k).wait_send()
        weights_forward(k).wait_send()
        weights_near(k).wait_send()

        @pl.when(lax.rem(k, 2) == inner)
        def _():
            inner_copy(k).wait_send()
            weights_over(k).wait_send()
            weights_inner(k).wait_send()

    @pl.when(zy < np_n)
    def _():
        @pl.loop(1, outer_n)
        def _(j):
            gather_copy(j).wait_send()

    @pl.loop(1, zy_n)
    def _(j):
        norm_out(j).wait_send()

    norm_first.wait_send()
    norm_last.wait_send()
    for one in [w_own, w_near, g_out, w_c, w_o]:
        one.wait()


def finish(
    np_n, pr, rpc,
    mq_hbm, oq_hbm, sq_hbm, mk_hbm, ok_hbm, sk_hbm, g_hbm, w_hbm, clip_ref,
    nmq_hbm, noq_hbm, nsq_hbm, nmk_hbm, nok_hbm, nsk_hbm, wq_hbm, wk_hbm,
    mq, oq, sq, mk, ok, sk, g, w, wq, wk, wk_rows, gk_rows, gk,
    in_sem, out_sem, more_sem, end_sem,
):
    tiles_all = rpc // RT
    tiles = pr // RT
    parts = 3 if tiles_all % 3 == 0 else 1
    step = tiles_all // parts
    half = CORES * rpc
    clip = clip_ref[0:1, 0:1]

    def block(n):
        return slice(n * step * RT, (n + 1) * step * RT)

    def q_in(n):
        return [
            pltpu.make_async_copy(src.at[block(n), :], dst.at[block(n), :], in_sem.at[n, i])
            for i, (src, dst) in enumerate([(mq_hbm, mq), (oq_hbm, oq), (sq_hbm, sq)])
        ]

    def q_out(n):
        return [
            pltpu.make_async_copy(src.at[block(n), :], dst.at[block(n), :], out_sem.at[n, i])
            for i, (src, dst) in enumerate([(mq, nmq_hbm), (oq, noq_hbm), (sq, nsq_hbm)])
        ]

    g_in = [pltpu.make_async_copy(g_hbm.at[a], g.at[a], more_sem.at[a]) for a in range(CORES)]
    w_in = [pltpu.make_async_copy(w_hbm.at[a], w.at[a], more_sem.at[CORES + a]) for a in range(2)]
    k_in = [
        pltpu.make_async_copy(src, dst, more_sem.at[CORES + 2 + i])
        for i, (src, dst) in enumerate([(mk_hbm, mk), (ok_hbm, ok), (sk_hbm, sk)])
    ]
    total = CORES * parts
    w_in[0].start()
    g_in[0].start()
    for n in range(total):
        for one in q_in(n):
            one.start()
        if n == 0:
            for one in w_in[1:] + g_in[1:]:
                one.start()
    for one in k_in:
        one.start()
    ends = []

    def end(i, src, dst):
        one = pltpu.make_async_copy(src, dst, end_sem.at[i])
        one.start()
        ends.append(one)

    def weights(xh):
        w_in[xh].wait()
        for core in range(CORES):

            @pl.loop(0, tiles_all, unroll=True)
            def _(i):
                row = pl.ds(pl.multiple_of(xh * half + core * rpc + i * RT, RT), RT)
                at = pl.ds(pl.multiple_of(lax.rem(i, tiles) * RT, RT), RT)
                q, k = split(w[xh, core, lax.div(i, tiles), at, :].astype(F32))
                wq[row, :] = q.astype(BF16)
                wk_rows[row, :] = k

        both = slice(xh * half, (xh + 1) * half)
        end(xh, wq.at[both, :], wq_hbm.at[both, :])

    def update(n):
        core = n // parts
        if n % parts == 0:
            g_in[core].wait()
        for one in q_in(n):
            one.wait()

        @pl.loop(n % parts * step, (n % parts + 1) * step, unroll=True)
        def _(i):
            row = pl.ds(pl.multiple_of(core * rpc + i * RT, RT), RT)
            at = pl.ds(pl.multiple_of(lax.rem(i, tiles) * RT, RT), RT)
            gsq, gsk = split(g[core, lax.div(i, tiles), at, :].astype(F32))
            mq[row, :], oq[row, :], sq[row, :] = adamw(gsq, mq[row, :], oq[row, :], sq[row, :], clip)
            gk_rows[row, :] = gsk

        for one in q_out(n):
            one.start()

    weights(0)
    update(0)
    weights(1)
    for lane in range(0, wk.shape[1], 128):
        lanes = slice(lane, min(lane + 128, wk.shape[1]))
        wk[:, lanes] = wk_rows[lanes, :].T.astype(BF16)
    end(2, wk, wk_hbm)
    for n in range(1, total):
        update(n)
    gk[...] = gk_rows[...].T
    for one in k_in:
        one.wait()

    @pl.loop(0, gk.shape[0] // RT, unroll=4)
    def _(i):
        row = pl.ds(pl.multiple_of(i * RT, RT), RT)
        mk[row, :], ok[row, :], sk[row, :] = adamw(gk[row, :], mk[row, :], ok[row, :], sk[row, :], clip)

    for i, (src, dst) in enumerate([(mk, nmk_hbm), (ok, nok_hbm), (sk, nsk_hbm)]):
        end(3 + i, src, dst)
    for n in range(total):
        for one in q_out(n):
            one.wait()
    for one in ends:
        one.wait()


def local(zy_n, grads_query, master_query, moment_query, second_query, grads_keys, master_keys, moment_keys, second_keys):
    half = master_query.shape[0]
    rpc = half // CORES
    tiles_all = rpc // RT
    per = -(-tiles_all // zy_n)
    np_n = -(-tiles_all // per)
    pr = per * RT
    keys = [master_keys, moment_keys, second_keys]
    states = [master_query, moment_query, second_query] + [a.T for a in keys]
    grads_keys = grads_keys.transpose(0, 2, 1)
    sem = lambda n: pltpu.SemaphoreType.DMA((n,))
    any_spec = pl.BlockSpec(memory_space=pl.ANY)
    sums, weights, clip = pl.pallas_call(
        functools.partial(kernel, zy_n, np_n, pr, rpc),
        out_shape=[
            jax.ShapeDtypeStruct((CORES, np_n, pr, WIDE), BF16),
            jax.ShapeDtypeStruct((2, CORES, np_n, pr, WIDE), BF16),
            jax.ShapeDtypeStruct((8, 128), F32),
        ],
        in_specs=[any_spec] * 8,
        out_specs=[any_spec, any_spec, pl.BlockSpec(memory_space=pltpu.VMEM)],
        scratch_shapes=[
            pltpu.VMEM(grads_query.shape, BF16),
            pltpu.VMEM(grads_keys.shape, BF16),
        ]
        + [pltpu.VMEM((rpc, D), F32)] * 3
        + [pltpu.VMEM(a.shape, F32) for a in states[3:] + keys]
        + [pltpu.VMEM((grads_keys.shape[2], grads_keys.shape[1]), F32)]
        + [
            pltpu.VMEM((np_n, 2, pr, WIDE), BF16),
            pltpu.VMEM((np_n, 2, pr, WIDE), BF16),
            pltpu.VMEM((np_n, pr, WIDE), BF16),
            pltpu.VMEM((np_n, pr, WIDE), BF16),
            pltpu.VMEM((np_n, pr, WIDE), BF16),
            pltpu.VMEM((zy_n, pr, WIDE), BF16),
            pltpu.VMEM((pr, WIDE), F32),
            pltpu.VMEM((CORES, np_n, pr, WIDE), BF16),
            pltpu.VMEM((2, CORES, np_n, pr, WIDE), BF16),
            pltpu.VMEM((3, 8, 128), F32),
            pltpu.VMEM((2 + zy_n, 8, 128), F32),
            sem(5), sem(6), sem(5),
            sem(np_n), sem(np_n), sem(np_n), sem(np_n), sem(np_n), sem(zy_n),
            sem(zy_n), sem(np_n), sem(np_n), sem(np_n), sem(np_n),
            sem(np_n), sem(np_n), sem(np_n), sem(np_n), sem(np_n), sem(np_n), sem(np_n), sem(2 + zy_n), sem(2 + zy_n),
        ],
        compiler_params=pltpu.CompilerParams(
            collective_id=0, has_side_effects=True, vmem_limit_bytes=56 << 20
        ),
    )(grads_query, *states[:3], grads_keys, *states[3:])
    parts = 3 if tiles_all % 3 == 0 else 1
    outs = pl.pallas_call(
        functools.partial(finish, np_n, pr, rpc),
        out_shape=[jax.ShapeDtypeStruct(a.shape, F32) for a in states]
        + [jax.ShapeDtypeStruct((2 * half, D), BF16), jax.ShapeDtypeStruct((KV, 2 * half), BF16)],
        in_specs=[any_spec] * 8 + [pl.BlockSpec(memory_space=pltpu.VMEM)],
        out_specs=[any_spec] * 8,
        scratch_shapes=[pltpu.VMEM(a.shape, F32) for a in states]
        + [
            pltpu.VMEM(sums.shape, BF16),
            pltpu.VMEM(weights.shape, BF16),
            pltpu.VMEM((2 * half, D), BF16),
            pltpu.VMEM((KV, 2 * half), BF16),
            pltpu.VMEM((2 * half, KV), F32),
            pltpu.VMEM((half, KV), F32),
            pltpu.VMEM((KV, half), F32),
            pltpu.SemaphoreType.DMA((CORES * parts, 3)),
            pltpu.SemaphoreType.DMA((CORES * parts, 3)),
            sem(CORES + 5), sem(6),
        ],
        compiler_params=pltpu.CompilerParams(vmem_limit_bytes=56 << 20),
    )(*states, sums, weights, clip)
    return (*outs[:3], outs[6], *[a.T for a in outs[3:6]], outs[7].T)


def solution(mesh):
    zy_n = mesh.shape["rep"] // CORES
    rows = P("shard", None)
    grads = P(("rep", "shard"), None, None)
    in_specs = (grads, rows, rows, rows, grads, rows, rows, rows)
    out_specs = (rows, rows, rows, P(), rows, rows, rows, P())
    return jax.shard_map(
        functools.partial(local, zy_n), mesh=mesh, in_specs=in_specs, out_specs=out_specs, check_vma=False
    )
```
